32 devices in a mesh: expert: 16 (over z, x, core), dp: 2 (over y).
Axes of the slice: x: 2, y: 2, z: 4, core: 2. Of those that a mesh axis runs over, the one named last changes fastest.
Arguments:
- tokens: bfloat16 [3072, 2048], P(('expert', 'dp')), may hold values from -6 to 6
- norm_gain: float32 [2048], replicated, may hold values from 0.1 to 1.9
- expert_ids: int32 [3072, 8], P(('expert', 'dp')), may hold values from 0 to 31, all different within a row; in each aligned block of 96 rows (0 to 95, 96 to 191, ...) at most 32 rows name the same one
- route_weights: float32 [3072, 8], P(('expert', 'dp')), may hold values from 0.05 to 1
- gate_weight: bfloat16 [32, 2048, 768], P('expert', 'dp'), may hold values from -0.125 to 0.125
- up_weight: bfloat16 [32, 2048, 768], P('expert', 'dp'), may hold values from -0.125 to 0.125
- down_weight: bfloat16 [32, 768, 2048], P('expert', 'dp'), may hold values from -0.21875 to 0.21875
- pair_list: int32 [16], replicated, may hold values from 0 to 15, as said below
Outputs:
- mixed: bfloat16 [3072, 2048], P(('expert', 'dp'))
- held_gate: bfloat16 [16, 2048, 768], P('expert', 'dp')
- held_up: bfloat16 [16, 2048, 768], P('expert', 'dp')
- held_down: bfloat16 [16, 768, 2048], P('expert', 'dp')
The draws below stay inside these ranges and needn't reach their ends.
Inputs may be any that keep to these rules, and one draw needn't show every extreme that they name: pair_list[pair_list[e]] = e, and pair_list[e] is e itself or differs from e in exactly one bit. `expert_ids`: each row names 8 different experts; among the rows of one device no expert is named more than 32 times, and in every draw some device's rows name one expert exactly 32 times.
All inputs are finite; a program needn't handle non-finite values.
Results may differ from the reference program's by a relative error of at most 0.0075.
Values may be sent and summed in bfloat16 or wider, within the bound.
A program may use at most 192 MiB of HBM per device.

```python
import math
import jax
import jax.numpy as jnp
import numpy as np
from jax import lax

D = 2048
FF = 768
TOP = 8
EXP_DEV = 2
TOK_DEV = 96
EXPERTS = 32
MOST = 32
TOKENS = 3072
BITS = 4
N_EXPERT = 16
N_DP = 2


def draw_pair_list(key, part):
    positions = jnp.arange(N_EXPERT, dtype=jnp.int32)
    partners = positions
    for bit_number in range(BITS):
        tosses = jax.random.randint(jax.random.fold_in(key, 17 + bit_number), (N_EXPERT,), 0, 4)
        counterpart = jnp.bitwise_xor(positions, 1 << bit_number)
        lowest = jnp.minimum(positions, counterpart)
        unmatched = partners == positions
        chosen = (tosses[lowest] == 0) & unmatched & unmatched[counterpart]
        partners = jnp.where(chosen, counterpart, partners)
    return partners.astype(jnp.int32)


def block_levels(own_key, shape, split, smallest, top_value):
    def one(axis_at, shards_of):
        steps = jax.random.uniform(jax.random.fold_in(jax.random.fold_in(own_key, 6), axis_at), (shards_of,), jnp.float32, smallest / len(split), top_value / len(split))
        return jnp.repeat(jnp.exp(steps), shape[axis_at] // shards_of).reshape((-1,) + (1,) * (len(shape) - axis_at - 1))

    level = one(*split[0])
    for cut in split[1:]:
        level = level * one(*cut)
    return level


def shared_out(own_key, own, number, rows, number_of, top, bound, skew):
    ranking = jax.random.permutation(own_key, number_of)
    packed, ordinary = portions_of(number_of, rows * top, bound, skew, True), portions_of(number_of, rows * top, bound, skew, False)
    places = jnp.arange(number_of)

    def named(sizes, rotation):
        used = int((sizes > 0).sum())
        fixed = max(1, used // 4)
        passed = fixed + (places - fixed + rotation * (used - fixed)) % max(1, number_of - fixed)
        return jnp.zeros((number_of,), jnp.int32).at[ranking[jnp.where(places < fixed, places, passed)]].set(jnp.asarray(sizes, jnp.int32))

    sizes = jnp.where(number % 4 == 0, named(packed, number // 4), named(ordinary, number - number // 4 - 1))
    mixed = jax.random.permutation(jax.random.fold_in(own, 3), number_of)
    donor, sink = mixed[0:number_of // 2 * 2:2], mixed[1:number_of // 2 * 2:2]
    room = jnp.minimum(sizes[donor] - 1, bound - sizes[sink]) // 2
    room = jnp.where((donor == ranking[0]) | (sink == ranking[0]) | (sizes[sink] == 0), 0, jnp.maximum(room, 0))
    passed = jax.random.randint(jax.random.fold_in(own, 4), (number_of // 2,), 0, 1 << 20) % (room + 1)
    sizes = sizes.at[donor].add(-passed).at[sink].add(passed)
    items = jnp.searchsorted(jnp.cumsum(sizes), jnp.arange(rows * top), side="right").astype(jnp.int32)
    listing = items.reshape(top, rows).T
    listing = listing[jax.random.permutation(jax.random.fold_in(own, 1), rows)]
    rotation = jax.random.randint(jax.random.fold_in(own, 2), (rows, 1), 0, top)
    return jnp.take_along_axis(listing, (jnp.arange(top)[None, :] + rotation) % top, axis=1)


def portions_of(number_of, total, reach, slope, full):
    loads = [(1 << 20) // math.isqrt(rank ** slope) + 1 for rank in range(1, number_of + 1)]
    largest = reach if full else min(reach, max(-(-total // number_of), total * loads[0] // sum(loads)))
    least = 1 if total - largest >= number_of - 1 else 0
    counts, spare = [largest] + [least] * (number_of - 1), total - largest - least * (number_of - 1)
    while spare > 0:
        candidates = [i for i in range(1, number_of) if counts[i] < largest] or [i for i in range(1, number_of) if counts[i] < reach]
        pool, budget = sum([loads[i] for i in candidates]), spare
        for i in candidates:
            extra = min(reach - counts[i], max(1, budget * loads[i] // pool), spare)
            counts[i] = counts[i] + extra
            spare = spare - extra
    return np.array(counts)


def normal_values(rng, shape, spread, most, split=(), kind=jnp.bfloat16):
    drawn = jax.random.normal(rng, shape, jnp.float32) * spread
    if len(split) > 0:
        drawn = block_levels(rng, shape, split, -0.22, 0.18) * drawn
    return jnp.clip(drawn, min=-most, max=most).astype(kind)


def setup_inputs(seed: int = 0) -> dict:
    splits = jax.random.split(jax.random.key(seed), 9)
    tokens = normal_values(splits[0], (TOKENS, D), 1.0, 6.0, ((0, 32),))
    norm_gain = jnp.clip(1.0 + 0.18 * jax.random.normal(splits[1], (D,), jnp.float32), 0.1, 1.9)
    expert_ids_keys = jax.random.split(jax.random.fold_in(splits[2], 1), TOKENS // TOK_DEV)
    expert_ids_turns = jax.random.permutation(jax.random.fold_in(splits[2], 3), TOKENS // TOK_DEV)
    expert_ids = jax.vmap(lambda own, number: shared_out(jax.random.fold_in(splits[2], 2), own, number, TOK_DEV, EXPERTS, TOP, MOST, 2))(expert_ids_keys, expert_ids_turns).reshape((TOKENS, TOP))
    route_weights = jnp.clip(0.05 + 0.95 * jax.random.uniform(splits[3], (TOKENS, TOP), jnp.float32) ** block_levels(splits[3], (TOKENS, TOP), ((0, 32),), -0.2, 0.2), 0.05, 1.0)
    gate_weight = normal_values(splits[4], (EXPERTS, D, FF), D ** -0.5, 0.125, ((0, 16), (1, 2)))
    up_weight = normal_values(splits[5], (EXPERTS, D, FF), D ** -0.5, 0.125, ((0, 16), (1, 2)))
    down_weight = normal_values(splits[6], (EXPERTS, FF, D), FF ** -0.5, 0.21875, ((0, 16), (1, 2)))
    pair_list = draw_pair_list(jax.random.fold_in(splits[8], 71), 0)
    return dict(tokens=tokens, norm_gain=norm_gain, expert_ids=expert_ids, route_weights=route_weights, gate_weight=gate_weight, up_weight=up_weight, down_weight=down_weight, pair_list=pair_list)


def reference(tokens, norm_gain, expert_ids, route_weights, gate_weight, up_weight, down_weight, pair_list):
    values = tokens.astype(jnp.float32)
    scale = lax.rsqrt(lax.optimization_barrier(jnp.mean(values * values, axis=-1, keepdims=True)) + 1e-06)
    normed = (values * scale * norm_gain).astype(jnp.bfloat16)
    flat_ids = expert_ids.reshape(-1)
    flat_weights = lax.optimization_barrier(route_weights.reshape(-1).astype(jnp.bfloat16)).astype(jnp.float32)
    capacity = N_EXPERT * N_DP * MOST

    def one_expert(expert, total):
        matching = flat_ids == expert
        chosen = jnp.nonzero(matching, size=capacity, fill_value=0)[0].astype(jnp.int32)
        number = jnp.sum(matching.astype(jnp.int32))
        valid = jnp.arange(capacity, dtype=jnp.int32) < number
        token_rows = (chosen // TOP).astype(jnp.int32)
        inputs = normed[token_rows]
        gate_act = jnp.dot(inputs, gate_weight[expert], preferred_element_type=jnp.float32)
        up_act = jnp.dot(inputs, up_weight[expert], preferred_element_type=jnp.float32)
        hidden = (jax.nn.silu(gate_act) * up_act).astype(jnp.bfloat16)
        result = jnp.dot(hidden, down_weight[expert], preferred_element_type=jnp.float32)
        result = lax.optimization_barrier(result.astype(jnp.bfloat16)).astype(jnp.float32)
        factor = jnp.where(valid, flat_weights[chosen], jnp.zeros((), jnp.float32))
        return total.at[token_rows].add(result * factor[:, None])
    total = lax.fori_loop(0, EXPERTS, one_expert, jnp.zeros((TOKENS, D), jnp.float32))
    mixed = total.astype(jnp.bfloat16)
    source = (EXP_DEV * pair_list).astype(jnp.int32)
    return (mixed, gate_weight[source], up_weight[source], down_weight[source])
```

```python
import functools

import jax
import jax.numpy as jnp
from jax import lax
from jax.experimental import pallas as pl
from jax.experimental.pallas import tpu as pltpu
from jax.sharding import PartitionSpec as P

F32 = jnp.float32
BF16 = jnp.bfloat16
MESH = pl.DeviceIdType.MESH
ANY = pl.BlockSpec(memory_space=pl.ANY)
INV = pl.BlockSpec(memory_space=pltpu.VMEM)


def bit_route(count, bit, cores):
    return [
        (e, e ^ (1 << bit)) for e in range(count) if e ^ (1 << bit) < count and (e & 1) in cores
    ]


def swap_branch(moves, count):
    def run(blocks, base, distance):
        arrived = [
            [lax.ppermute(b, "expert", bit_route(count, bit, cores)) for b in blocks]
            for bit, cores in moves
        ]
        out = base
        for (bit, _), got in zip(moves, arrived):
            out = [jnp.where(distance == (1 << bit), a, o) for a, o in zip(got, out)]
        return tuple(out)

    return run


def swap(blocks, base, pair_list, count, always, bits):
    mine = lax.axis_index("expert")
    places = jnp.arange(count, dtype=jnp.int32)
    distances = jnp.bitwise_xor(pair_list, places)
    distance = jnp.bitwise_xor(pair_list[mine], mine)
    choice = jnp.int32(0)
    for n, bit in enumerate(bits):
        for core in range(2):
            used = jnp.any((distances == (1 << bit)) & (places & 1 == core)).astype(jnp.int32)
            choice = choice + (used << (2 * n + core))
    branches = []
    for mask in range(1 << (2 * len(bits))):
        moves = [(bit, (0, 1)) for bit in always]
        for n, bit in enumerate(bits):
            cores = tuple(c for c in range(2) if mask >> (2 * n + c) & 1)
            if cores:
                moves.append((bit, cores))
        branches.append(swap_branch(moves, count))
    return list(lax.switch(choice, branches, list(blocks), list(base), distance))


def placing_of(ids, parity, count, per_device, capacity):
    rows = ids.shape[0]
    experts = jnp.arange(count, dtype=jnp.int32) * per_device + parity
    equal = ids[:, :, None] == experts[None, None, :]
    member = jnp.any(equal, axis=1)
    lower = jnp.tril(jnp.ones((rows, rows), BF16), -1)
    rank = jnp.dot(lower, member.astype(BF16), preferred_element_type=F32).astype(jnp.int32)
    rank = jnp.where(member, rank, -1)
    slots = jnp.arange(capacity, dtype=jnp.int32)
    hit = rank.T[:, None, :] == slots[None, :, None]
    return equal, hit


def wide_body(
    tokens, norm_gain, expert_ids, route_weights, gate_weight, up_weight, down_weight, pair_list
):
    count = lax.axis_size("expert")
    dp = lax.axis_size("dp")
    per_device = gate_weight.shape[0]
    group = per_device if dp % per_device == 0 else 1
    experts_all = count * per_device
    rows, top = expert_ids.shape
    width = tokens.shape[1]
    capacity = max(2, 4 * rows * top // (3 * experts_all))
    d = lax.axis_index("dp")
    parity = d % group

    values = tokens.astype(F32)
    scale = lax.rsqrt(jnp.mean(values * values, axis=-1, keepdims=True) + 1e-06)
    normed = (values * scale * norm_gain).astype(BF16)
    route_bf = route_weights.astype(BF16)

    def in_group(block, shift):
        if shift % group == 0:
            return block
        route = [(i, i // group * group + (i % group + shift) % group) for i in range(dp)]
        return lax.ppermute(block, "dp", route)

    token_sets = [
        (in_group(normed, s), in_group(expert_ids, s), in_group(route_bf, s)) for s in range(group)
    ]
    token_sets, weights = lax.optimization_barrier(
        (token_sets, (gate_weight, up_weight, down_weight))
    )

    def shards(weight):
        out = []
        for s in range(dp):
            sent = lax.dynamic_index_in_dim(weight, (d + s) % group, 0, keepdims=False)
            if s:
                sent = lax.ppermute(sent, "dp", [(i, (i + s) % dp) for i in range(dp)])
            out.append(sent)
        return out

    gates, ups, downs = [shards(w) for w in weights]

    outgoing, weightings = [], []
    for normed_s, ids_s, route_s in token_sets:
        equal, hit = placing_of(ids_s, parity, count, per_device, capacity)
        picked = jnp.dot(
            hit.reshape(count * capacity, rows).astype(BF16), normed_s, preferred_element_type=F32
        ).astype(BF16)
        outgoing.append(picked.reshape(count, capacity, width))
        factor = jnp.sum(jnp.where(equal, route_s[:, :, None], jnp.zeros((), BF16)), axis=1)
        weightings.append(
            jnp.where(hit, factor.T[:, None, :], jnp.zeros((), BF16)).reshape(
                count * capacity, rows
            )
        )
    outgoing = jnp.concatenate(outgoing, axis=1)
    bit_total = count.bit_length() - 1
    firsts = [gate_weight[0], up_weight[0], down_weight[0]]
    early = list(range(1, min(3, bit_total)))
    late = list(range(3, bit_total))
    outgoing, pairs = lax.optimization_barrier((outgoing, pair_list))
    received = lax.all_to_all(outgoing, "expert", split_axis=0, concat_axis=0, tiled=True)
    half_held = swap(firsts, firsts, pairs, count, [], early)
    received, half_held = lax.optimization_barrier((received, half_held))
    columns = received.reshape(count * group * capacity, width)

    def times(x, parts):
        size = parts[0].shape[0]
        total = None
        for s, part in enumerate(parts):
            at = (d - s) % dp
            piece = lax.dynamic_slice_in_dim(x, at * size, size, axis=1)
            term = jnp.dot(piece, part, preferred_element_type=F32)
            total = term if total is None else total + term
        return total

    hidden = (jax.nn.silu(times(columns, gates)) * times(columns, ups)).astype(BF16)
    expert_out = times(hidden, downs).astype(BF16)
    expert_out, pairs = lax.optimization_barrier((expert_out, pairs))
    held = swap(firsts, half_held, pairs, count, [0], late)
    returned = lax.all_to_all(
        expert_out.reshape(count, group * capacity, width),
        "expert",
        split_axis=0,
        concat_axis=0,
        tiled=True,
    )
    returned, held = lax.optimization_barrier((returned, held))
    total = None
    for s in range(group):
        part = returned[:, s * capacity : (s + 1) * capacity].reshape(count * capacity, width)
        mix = jnp.einsum("sr,sd->rd", weightings[s], part, preferred_element_type=F32)
        if s:
            mix = in_group(mix.astype(BF16), group - s).astype(F32)
        total = mix if total is None else total + mix
    return (total.astype(BF16), held[0][None], held[1][None], held[2][None])


def flip(index, step):
    return index + step * (1 - 2 * ((index // step) % 2))


def pick(table, index):
    value = jnp.int32(table[0])
    for n in range(1, len(table)):
        value = value + jnp.int32(table[n] - table[0]) * (1 - jnp.minimum(jnp.abs(index - n), 1))
    return value


def near_first(places):
    return [sorted(range(places), key=lambda p: (abs(p - at), p)) for at in range(places)]


def greet(lines, z, e, d, moves):
    barrier = pltpu.get_barrier_semaphore()

    def signal(to_e, to_d):
        pl.semaphore_signal(barrier, inc=1, device_id=(to_e, to_d), device_id_type=MESH)

    signal(e, 1 - d)
    for offset in range(1, 4):
        signal(beside(e, offset), d)
    total = 4 + jnp.minimum(z, 1) + jnp.minimum(lines - 1 - z, 1)

    @pl.when(z > 0)
    def _():
        signal(e - 4, d)

    @pl.when(z < lines - 1)
    def _():
        signal(e + 4, d)

    for bit, _ in moves:
        if bit > 2:
            signal(flip(e, 1 << bit), d)
            total = total + 1
    pl.semaphore_wait(barrier, total)


def beside(e, offset):
    for bit in range(2):
        if offset >> bit & 1:
            e = flip(e, 1 << bit)
    return e


def remote(src, dst, send, recv, to_e, to_d):
    return pltpu.make_async_remote_copy(
        src_ref=src,
        dst_ref=dst,
        send_sem=send,
        recv_sem=recv,
        device_id=(to_e, to_d),
        device_id_type=MESH,
    )


def for_cores(cores, c, act):
    if len(cores) == 2:
        act()
    else:
        pl.when(c == cores[0])(act)


def swap_copies(part, parts, srcs, dsts, send, recv, moves, e, d):
    out = []
    for n, (bit, cores) in enumerate(moves):
        for k, (src, dst) in enumerate(zip(srcs, dsts)):
            size = src.shape[1] // parts
            rows = pl.ds(pl.multiple_of(part * size, size), size)
            slot = (part, n * len(srcs) + k)
            copy = remote(
                src.at[0, rows],
                dst.at[bit, rows],
                send.at[slot],
                recv.at[slot],
                flip(e, 1 << bit),
                d,
            )
            out.append((copy, cores))
    return out


def spread_kernel(
    lines, cap, moves, block, meta, gate, up, down,
    taken, mats, far_gate, far_up, far_down, got_gate, got_up,
    held, metas, chosen,
    o_sem, y_send, y_recv, z_send, z_recv, x_send, x_recv, s_send, s_recv,
):
    e, d = lax.axis_index("expert"), lax.axis_index("dp")
    z, c = e // 4, e % 2
    rows = block.shape[0]
    lanes = meta.shape[1]
    top = meta.shape[0] // 2
    blocks = 2 * lines
    order = near_first(lines)
    greet(lines, z, e, d, moves)

    def across():
        return [
            remote(src, dst, y_send.at[n], y_recv.at[n], e, 1 - d)
            for n, (src, dst) in enumerate(
                [
                    (block, held.at[z, d]),
                    (meta, metas.at[z, d]),
                    (gate.at[1 - d], far_gate),
                    (up.at[1 - d], far_up),
                    (down.at[1 - d], far_down),
                ]
            )
        ]

    def own():
        return [
            pltpu.make_async_copy(src, dst, o_sem.at[n])
            for n, (src, dst) in enumerate([(block, held.at[z, d]), (meta, metas.at[z, d])])
        ]

    for copy in across() + own():
        copy.start()
    for copy in own():
        copy.wait()

    def along(way, at, dd, tokens, tags):
        to = e + 4 if way else e - 4
        return [
            remote(tokens, held.at[at, dd], z_send.at[way, at, dd, 0], z_recv.at[at, dd, 0], to, d),
            remote(tags, metas.at[at, dd], z_send.at[way, at, dd, 1], z_recv.at[at, dd, 1], to, d),
        ]

    def sideways(at, dd, n):
        return [
            remote(
                chosen.at[n, offset - 1],
                taken.at[offset, at, dd],
                x_send.at[n, offset - 1],
                x_recv.at[at, dd, offset - 1],
                beside(e, offset),
                d,
            )
            for offset in range(1, 4)
        ]

    def swaps(part):
        return swap_copies(
            part, blocks, [gate, up], [got_gate, got_up], s_send, s_recv, moves, e, d
        )

    upper = (
        lax.broadcasted_iota(jnp.int32, (lanes, lanes), 0)
        < lax.broadcasted_iota(jnp.int32, (lanes, lanes), 1)
    ).astype(F32).astype(BF16)
    slots = lax.broadcasted_iota(jnp.int32, (cap, lanes), 0).astype(F32)
    places = lax.broadcasted_iota(jnp.int32, (8, lanes), 0)

    def where_at(n):
        near = n // 2
        at = jnp.int32(0)
        for k in range(lines):
            at = at + (1 - jnp.minimum(jnp.abs(near - k), 1)) * pick(
                [order[p][k] for p in range(lines)], z
            )
        return at, (d + n % 2) % 2

    def step(n, _):
        at, dd = where_at(n)

        @pl.when(n == 1)
        def _():
            for copy in across()[:2]:
                copy.wait_recv()

        @pl.when(n > 1)
        def _():
            for copy in along(1, at, dd, held.at[at, dd], metas.at[at, dd]):
                copy.wait_recv()

        @pl.when(jnp.logical_and(at <= z, z < lines - 1))
        def _():
            for copy in along(1, at, dd, held.at[at, dd], metas.at[at, dd]):
                copy.start()

        @pl.when(jnp.logical_and(at >= z, z > 0))
        def _():
            for copy in along(0, at, dd, held.at[at, dd], metas.at[at, dd]):
                copy.start()

        tags = metas[at, dd].astype(F32)
        ids, parts = tags[:top], tags[top:]
        member = jnp.zeros((8, lanes), F32)
        factors = []
        for offset in range(4):
            expert = (2 * beside(e, offset) + d).astype(F32)
            same = ids == expert
            row = jnp.max(jnp.where(same, 1.0, 0.0), axis=0, keepdims=True)
            factors.append(jnp.sum(jnp.where(same, parts, 0.0), axis=0, keepdims=True))
            member = jnp.where(places == offset, row, member)
        rank = jnp.dot(member.astype(BF16), upper, preferred_element_type=F32)
        hits, mixes = [], []
        for offset in range(4):
            hit = jnp.logical_and(
                rank[offset : offset + 1] == slots, member[offset : offset + 1] > 0.5
            )
            hits.append(jnp.where(hit, 1.0, 0.0))
            mixes.append(jnp.where(hit, factors[offset], 0.0))
        hit = jnp.concatenate(hits, axis=0).astype(BF16)
        mats[at, dd] = jnp.transpose(jnp.concatenate(mixes, axis=0)).astype(BF16)
        picked = jnp.dot(hit[:, :rows], held[at, dd], preferred_element_type=F32).astype(BF16)
        taken[0, at, dd] = picked[:cap]
        for offset in range(1, 4):
            chosen[n, offset - 1] = picked[offset * cap : (offset + 1) * cap]
        for copy in sideways(at, dd, n):
            copy.start()
        for copy, cores in swaps(n):
            for_cores(cores, c, copy.start)
        return 0

    lax.fori_loop(0, blocks, step, 0)

    def finish(n, _):
        at, dd = where_at(n)

        @pl.when(jnp.logical_and(at <= z, z < lines - 1))
        def _():
            for copy in along(1, at, dd, held.at[at, dd], metas.at[at, dd]):
                copy.wait_send()

        @pl.when(jnp.logical_and(at >= z, z > 0))
        def _():
            for copy in along(0, at, dd, held.at[at, dd], metas.at[at, dd]):
                copy.wait_send()

        for copy in sideways(at, dd, n):
            copy.wait()
        for copy, cores in swaps(n):
            for_cores(cores, c, copy.wait)
        return 0

    lax.fori_loop(0, blocks, finish, 0)
    last = across()
    for copy in last[:2]:
        copy.wait_send()
    for copy in last[2:]:
        copy.wait()


def spread(lines, cap, moves, key, block, meta, gate, up, down, bits):
    rows, width = block.shape
    lanes = meta.shape[1]
    blocks = 2 * lines
    half, hidden = gate.shape[1:]
    return pl.pallas_call(
        functools.partial(spread_kernel, lines, cap, moves),
        name="spread",
        out_shape=(
            jax.ShapeDtypeStruct((4, lines, 2, cap, width), BF16),
            jax.ShapeDtypeStruct((lines, 2, lanes, 4 * cap), BF16),
            jax.ShapeDtypeStruct(gate.shape[1:], BF16),
            jax.ShapeDtypeStruct(up.shape[1:], BF16),
            jax.ShapeDtypeStruct(down.shape[1:], BF16),
            jax.ShapeDtypeStruct((bits, half, hidden), BF16),
            jax.ShapeDtypeStruct((bits, half, hidden), BF16),
        ),
        in_specs=[INV, INV, ANY, ANY, ANY],
        out_specs=(INV, INV, ANY, ANY, ANY, ANY, ANY),
        scratch_shapes=[
            pltpu.VMEM((lines, 2, rows, width), BF16),
            pltpu.VMEM((lines, 2, meta.shape[0], lanes), BF16),
            pltpu.VMEM((blocks, 3, cap, width), BF16),
            pltpu.SemaphoreType.DMA((2,)),
            pltpu.SemaphoreType.DMA((5,)),
            pltpu.SemaphoreType.DMA((5,)),
            pltpu.SemaphoreType.DMA((2, lines, 2, 2)),
            pltpu.SemaphoreType.DMA((lines, 2, 2)),
            pltpu.SemaphoreType.DMA((blocks, 3)),
            pltpu.SemaphoreType.DMA((lines, 2, 3)),
            pltpu.SemaphoreType.DMA((blocks, 2 * len(moves))),
            pltpu.SemaphoreType.DMA((blocks, 2 * len(moves))),
        ],
        compiler_params=pltpu.CompilerParams(
            collective_id=key, has_side_effects=True, vmem_limit_bytes=48 << 20
        ),
    )(block, meta, gate, up, down)


def gather_kernel(
    lines, cap, moves, outs, mats, down,
    mixed, got_down,
    back, total, held, from_left, from_right, other,
    l_sem, x_send, x_recv, z_send, z_recv, y_send, y_recv, s_send, s_recv,
):
    e, d = lax.axis_index("expert"), lax.axis_index("dp")
    z, c = e // 4, e % 2
    rows = mixed.shape[0]
    width = mixed.shape[1]
    blocks = 2 * lines
    order = [list(reversed(o)) for o in near_first(lines)]
    greet(lines, z, e, d, moves)

    def where_at(n):
        far = n // 2
        at = jnp.int32(0)
        for k in range(lines):
            at = at + (1 - jnp.minimum(jnp.abs(far - k), 1)) * pick(
                [order[p][k] for p in range(lines)], z
            )
        return at, (d + 1 + n % 2) % 2

    def sideways(at, dd):
        return [
            remote(
                outs.at[offset, at, dd],
                back.at[at, dd, offset],
                x_send.at[at, dd, offset - 1],
                x_recv.at[at, dd, offset - 1],
                beside(e, offset),
                d,
            )
            for offset in range(1, 4)
        ]

    def local(at, dd):
        return pltpu.make_async_copy(outs.at[0, at, dd], back.at[at, dd, 0], l_sem.at[at, dd])

    def along(way, at, dd):
        to = e + 4 if way else e - 4
        land = from_left if way else from_right
        return remote(
            held.at[at, dd], land.at[at, dd], z_send.at[at, dd], z_recv.at[way, at, dd], to, d
        )

    def swaps(part):
        return swap_copies(part, blocks, [down], [got_down], s_send, s_recv, moves, e, d)

    def across():
        return remote(held.at[z, 1 - d], other, y_send, y_recv, e, 1 - d)

    def begin(n, _):
        at, dd = where_at(n)
        local(at, dd).start()
        for copy in sideways(at, dd):
            copy.start()
        return 0

    lax.fori_loop(0, blocks, begin, 0)

    def step(n, _):
        at, dd = where_at(n)
        local(at, dd).wait()
        for copy in sideways(at, dd):
            copy.wait()
        total[...] = jnp.dot(
            mats[at, dd][:rows],
            back[at, dd].reshape(4 * cap, width),
            preferred_element_type=F32,
        )

        @pl.when(jnp.logical_and(at >= z, z > 0))
        def _():
            along(1, at, dd).wait_recv()
            total[...] += from_left[at, dd].astype(F32)

        @pl.when(jnp.logical_and(at <= z, z < lines - 1))
        def _():
            along(0, at, dd).wait_recv()
            total[...] += from_right[at, dd].astype(F32)

        held[at, dd] = total[...].astype(BF16)

        @pl.when(at > z)
        def _():
            along(1, at, dd).start()

        @pl.when(at < z)
        def _():
            along(0, at, dd).start()

        @pl.when(n == blocks - 2)
        def _():
            across().start()

        for copy, cores in swaps(n):
            for_cores(cores, c, copy.start)
        return 0

    lax.fori_loop(0, blocks, step, 0)
    across().wait()
    mixed[...] = (total[...] + other[...].astype(F32)).astype(BF16)

    def finish(n, _):
        at, dd = where_at(n)

        @pl.when(at > z)
        def _():
            along(1, at, dd).wait_send()

        @pl.when(at < z)
        def _():
            along(0, at, dd).wait_send()

        for copy, cores in swaps(n):
            for_cores(cores, c, copy.wait)
        return 0

    lax.fori_loop(0, blocks, finish, 0)


def gather(lines, cap, moves, key, outs, mats, down, rows, bits):
    width = outs.shape[-1]
    blocks = 2 * lines
    return pl.pallas_call(
        functools.partial(gather_kernel, lines, cap, moves),
        name="gather",
        out_shape=(
            jax.ShapeDtypeStruct((rows, width), BF16),
            jax.ShapeDtypeStruct((bits,) + down.shape[1:], BF16),
        ),
        in_specs=[INV, INV, ANY],
        out_specs=(INV, ANY),
        scratch_shapes=[
            pltpu.VMEM((lines, 2, 4, cap, width), BF16),
            pltpu.VMEM((rows, width), F32),
            pltpu.VMEM((lines, 2, rows, width), BF16),
            pltpu.VMEM((lines, 2, rows, width), BF16),
            pltpu.VMEM((lines, 2, rows, width), BF16),
            pltpu.VMEM((rows, width), BF16),
            pltpu.SemaphoreType.DMA((lines, 2)),
            pltpu.SemaphoreType.DMA((lines, 2, 3)),
            pltpu.SemaphoreType.DMA((lines, 2, 3)),
            pltpu.SemaphoreType.DMA((lines, 2)),
            pltpu.SemaphoreType.DMA((2, lines, 2)),
            pltpu.SemaphoreType.DMA,
            pltpu.SemaphoreType.DMA,
            pltpu.SemaphoreType.DMA((blocks, len(moves))),
            pltpu.SemaphoreType.DMA((blocks, len(moves))),
        ],
        compiler_params=pltpu.CompilerParams(
            collective_id=key, has_side_effects=True, vmem_limit_bytes=48 << 20
        ),
    )(outs, mats, down)


def square_body(
    tokens, norm_gain, expert_ids, route_weights, gate_weight, up_weight, down_weight, pair_list
):
    count = lax.axis_size("expert")
    dp = lax.axis_size("dp")
    e, d = lax.axis_index("expert"), lax.axis_index("dp")
    per_device = gate_weight.shape[0]
    rows, top = expert_ids.shape
    width = tokens.shape[1]
    lines = count // 4
    cap = 4 * rows * top // (3 * count * per_device)
    bits = count.bit_length() - 1
    lanes = -(-rows // 128) * 128

    values = tokens.astype(F32)
    scale = lax.rsqrt(jnp.mean(values * values, axis=-1, keepdims=True) + 1e-06)
    normed = (values * scale * norm_gain).astype(BF16)
    meta = jnp.concatenate([expert_ids.astype(BF16), route_weights.astype(BF16)], axis=1)
    meta = jnp.pad(meta.T, ((0, 0), (0, lanes - rows)), constant_values=-1)

    places = jnp.arange(count, dtype=jnp.int32)
    distances = jnp.bitwise_xor(pair_list, places)
    choice = jnp.int32(0)
    for n, bit in enumerate(range(1, bits)):
        choice = choice + (jnp.any(distances == (1 << bit)).astype(jnp.int32) << n)
    move_sets = []
    for mask in range(1 << (bits - 1)):
        move_sets.append(
            [(0, (0, 1))] + [(n + 1, (0, 1)) for n in range(bits - 1) if mask >> n & 1]
        )

    def first(moves, key):
        return lambda *args: spread(lines, cap, moves, key, *args, bits)

    taken, mats, far_gate, far_up, far_down, got_gate, got_up = lax.switch(
        choice,
        [first(moves, key) for key, moves in enumerate(move_sets)],
        normed, meta, gate_weight, up_weight, down_weight,
    )
    columns = taken.reshape(-1, width)

    def times(x, weight, far):
        size = far.shape[0]
        near = lax.dynamic_index_in_dim(weight, d, 0, keepdims=False)
        total = None
        for at, part in ((d, near), (1 - d, far)):
            piece = lax.dynamic_slice_in_dim(x, at * size, size, axis=1)
            term = jnp.dot(piece, part, preferred_element_type=F32)
            total = term if total is None else total + term
        return total

    hidden = (
        jax.nn.silu(times(columns, gate_weight, far_gate)) * times(columns, up_weight, far_up)
    ).astype(BF16)
    outs = times(hidden, down_weight, far_down).astype(BF16).reshape(taken.shape)

    def second(moves, key):
        return lambda *args: gather(lines, cap, moves, key, *args, rows, bits)

    mixed, got_down = lax.switch(
        choice,
        [second(moves, len(move_sets) + key) for key, moves in enumerate(move_sets)],
        outs, mats, down_weight,
    )
    distance = jnp.bitwise_xor(pair_list[e], e)
    slot = jnp.int32(0)
    for bit in range(1, bits):
        slot = slot + jnp.where(distance >= (1 << bit), 1, 0)

    def held(own, got):
        return jnp.where(distance == 0, own[:1], lax.dynamic_slice_in_dim(got, slot, 1, 0))

    return (
        mixed,
        held(gate_weight, got_gate),
        held(up_weight, got_up),
        held(down_weight, got_down),
    )


def body(*args):
    dp, count = lax.axis_size("dp"), lax.axis_size("expert")
    per_device = args[4].shape[0]
    rows, top = args[2].shape
    square = dp == 2 and per_device == 2 and count % 4 == 0 and rows * top % (3 * count) == 0
    return square_body(*args) if square else wide_body(*args)


def solution(mesh):
    in_specs = (
        P(("expert", "dp"), None),
        P(),
        P(("expert", "dp"), None),
        P(("expert", "dp"), None),
        P("expert", "dp", None),
        P("expert", "dp", None),
        P("expert", "dp", None),
        P(),
    )
    out_specs = (
        P(("expert", "dp"), None),
        P("expert", "dp", None),
        P("expert", "dp", None),
        P("expert", "dp", None),
    )
    return jax.shard_map(body, mesh=mesh, in_specs=in_specs, out_specs=out_specs, check_vma=False)
```

```python
import functools

import jax
import jax.numpy as jnp
from jax import lax
from jax.experimental import pallas as pl
from jax.experimental.pallas import tpu as pltpu
from jax.sharding import PartitionSpec as P

F32 = jnp.float32
BF16 = jnp.bfloat16
MESH = pl.DeviceIdType.MESH
ANY = pl.BlockSpec(memory_space=pl.ANY)
INV = pl.BlockSpec(memory_space=pltpu.VMEM)


def bit_route(count, bit, cores):
    return [
        (e, e ^ (1 << bit)) for e in range(count) if e ^ (1 << bit) < count and (e & 1) in cores
    ]


def swap_branch(moves, count):
    def run(blocks, base, distance):
        arrived = [
            [lax.ppermute(b, "expert", bit_route(count, bit, cores)) for b in blocks]
            for bit, cores in moves
        ]
        out = base
        for (bit, _), got in zip(moves, arrived):
            out = [jnp.where(distance == (1 << bit), a, o) for a, o in zip(got, out)]
        return tuple(out)

    return run


def swap(blocks, base, pair_list, count, always, bits):
    mine = lax.axis_index("expert")
    places = jnp.arange(count, dtype=jnp.int32)
    distances = jnp.bitwise_xor(pair_list, places)
    distance = jnp.bitwise_xor(pair_list[mine], mine)
    choice = jnp.int32(0)
    for n, bit in enumerate(bits):
        for core in range(2):
            used = jnp.any((distances == (1 << bit)) & (places & 1 == core)).astype(jnp.int32)
            choice = choice + (used << (2 * n + core))
    branches = []
    for mask in range(1 << (2 * len(bits))):
        moves = [(bit, (0, 1)) for bit in always]
        for n, bit in enumerate(bits):
            cores = tuple(c for c in range(2) if mask >> (2 * n + c) & 1)
            if cores:
                moves.append((bit, cores))
        branches.append(swap_branch(moves, count))
    return list(lax.switch(choice, branches, list(blocks), list(base), distance))


def placing_of(ids, parity, count, per_device, capacity):
    rows = ids.shape[0]
    experts = jnp.arange(count, dtype=jnp.int32) * per_device + parity
    equal = ids[:, :, None] == experts[None, None, :]
    member = jnp.any(equal, axis=1)
    lower = jnp.tril(jnp.ones((rows, rows), BF16), -1)
    rank = jnp.dot(lower, member.astype(BF16), preferred_element_type=F32).astype(jnp.int32)
    rank = jnp.where(member, rank, -1)
    slots = jnp.arange(capacity, dtype=jnp.int32)
    hit = rank.T[:, None, :] == slots[None, :, None]
    return equal, hit


def wide_body(
    tokens, norm_gain, expert_ids, route_weights, gate_weight, up_weight, down_weight, pair_list
):
    count = lax.axis_size("expert")
    dp = lax.axis_size("dp")
    per_device = gate_weight.shape[0]
    group = per_device if dp % per_device == 0 else 1
    experts_all = count * per_device
    rows, top = expert_ids.shape
    width = tokens.shape[1]
    capacity = max(2, 4 * rows * top // (3 * experts_all))
    d = lax.axis_index("dp")
    parity = d % group

    values = tokens.astype(F32)
    scale = lax.rsqrt(jnp.mean(values * values, axis=-1, keepdims=True) + 1e-06)
    normed = (values * scale * norm_gain).astype(BF16)
    route_bf = route_weights.astype(BF16)

    def in_group(block, shift):
        if shift % group == 0:
            return block
        route = [(i, i // group * group + (i % group + shift) % group) for i in range(dp)]
        return lax.ppermute(block, "dp", route)

    token_sets = [
        (in_group(normed, s), in_group(expert_ids, s), in_group(route_bf, s)) for s in range(group)
    ]
    token_sets, weights = lax.optimization_barrier(
        (token_sets, (gate_weight, up_weight, down_weight))
    )

    def shards(weight):
        out = []
        for s in range(dp):
            sent = lax.dynamic_index_in_dim(weight, (d + s) % group, 0, keepdims=False)
            if s:
                sent = lax.ppermute(sent, "dp", [(i, (i + s) % dp) for i in range(dp)])
            out.append(sent)
        return out

    gates, ups, downs = [shards(w) for w in weights]

    outgoing, weightings = [], []
    for normed_s, ids_s, route_s in token_sets:
        equal, hit = placing_of(ids_s, parity, count, per_device, capacity)
        picked = jnp.dot(
            hit.reshape(count * capacity, rows).astype(BF16), normed_s, preferred_element_type=F32
        ).astype(BF16)
        outgoing.append(picked.reshape(count, capacity, width))
        factor = jnp.sum(jnp.where(equal, route_s[:, :, None], jnp.zeros((), BF16)), axis=1)
        weightings.append(
            jnp.where(hit, factor.T[:, None, :], jnp.zeros((), BF16)).reshape(
                count * capacity, rows
            )
        )
    outgoing = jnp.concatenate(outgoing, axis=1)
    bit_total = count.bit_length() - 1
    firsts = [gate_weight[0], up_weight[0], down_weight[0]]
    early = list(range(1, min(3, bit_total)))
    late = list(range(3, bit_total))
    outgoing, pairs = lax.optimization_barrier((outgoing, pair_list))
    received = lax.all_to_all(outgoing, "expert", split_axis=0, concat_axis=0, tiled=True)
    half_held = swap(firsts, firsts, pairs, count, [], early)
    received, half_held = lax.optimization_barrier((received, half_held))
    columns = received.reshape(count * group * capacity, width)

    def times(x, parts):
        size = parts[0].shape[0]
        total = None
        for s, part in enumerate(parts):
            at = (d - s) % dp
            piece = lax.dynamic_slice_in_dim(x, at * size, size, axis=1)
            term = jnp.dot(piece, part, preferred_element_type=F32)
            total = term if total is None else total + term
        return total

    hidden = (jax.nn.silu(times(columns, gates)) * times(columns, ups)).astype(BF16)
    expert_out = times(hidden, downs).astype(BF16)
    expert_out, pairs = lax.optimization_barrier((expert_out, pairs))
    held = swap(firsts, half_held, pairs, count, [0], late)
    returned = lax.all_to_all(
        expert_out.reshape(count, group * capacity, width),
        "expert",
        split_axis=0,
        concat_axis=0,
        tiled=True,
    )
    returned, held = lax.optimization_barrier((returned, held))
    total = None
    for s in range(group):
        part = returned[:, s * capacity : (s + 1) * capacity].reshape(count * capacity, width)
        mix = jnp.einsum("sr,sd->rd", weightings[s], part, preferred_element_type=F32)
        if s:
            mix = in_group(mix.astype(BF16), group - s).astype(F32)
        total = mix if total is None else total + mix
    return (total.astype(BF16), held[0][None], held[1][None], held[2][None])


def flip(index, step):
    return index + step * (1 - 2 * ((index // step) % 2))


def pick(table, index):
    value = jnp.int32(table[0])
    for n in range(1, len(table)):
        value = value + jnp.int32(table[n] - table[0]) * (1 - jnp.minimum(jnp.abs(index - n), 1))
    return value


def near_first(places):
    return [sorted(range(places), key=lambda p: (abs(p - at), p)) for at in range(places)]


def greet(lines, z, e, d, moves):
    barrier = pltpu.get_barrier_semaphore()

    def signal(to_e, to_d):
        pl.semaphore_signal(barrier, inc=1, device_id=(to_e, to_d), device_id_type=MESH)

    signal(e, 1 - d)
    for offset in range(1, 4):
        signal(beside(e, offset), d)
    total = 4 + jnp.minimum(z, 1) + jnp.minimum(lines - 1 - z, 1)

    @pl.when(z > 0)
    def _():
        signal(e - 4, d)

    @pl.when(z < lines - 1)
    def _():
        signal(e + 4, d)

    for bit, _ in moves:
        if bit > 2:
            signal(flip(e, 1 << bit), d)
            total = total + 1
    pl.semaphore_wait(barrier, total)


def beside(e, offset):
    for bit in range(2):
        if offset >> bit & 1:
            e = flip(e, 1 << bit)
    return e


def remote(src, dst, send, recv, to_e, to_d):
    return pltpu.make_async_remote_copy(
        src_ref=src,
        dst_ref=dst,
        send_sem=send,
        recv_sem=recv,
        device_id=(to_e, to_d),
        device_id_type=MESH,
    )


def for_cores(cores, c, act):
    if len(cores) == 2:
        act()
    else:
        pl.when(c == cores[0])(act)


def layer_kernel(
    lines, cap, chunks, moves, block, meta, gate, up, down,
    mixed, got_gate, got_up, got_down,
    held, metas, chosen, taken, mats, all_gate, all_up, all_down, gates, hidden,
    outs, back, sums, from_left, from_right, total, other,
    o_sem, y_send, y_recv, z_send, z_recv, x_send, x_recv,
    b_sem, b_send, b_recv, r_send, r_recv, m_send, m_recv, s_send, s_recv,
):
    e, d = lax.axis_index("expert"), lax.axis_index("dp")
    z, c = e // 4, e % 2
    rows, width = block.shape
    lanes = meta.shape[1]
    top = meta.shape[0] // 2
    blocks = 2 * lines
    span = width // chunks
    order = near_first(lines)
    greet(lines, z, e, d, moves)

    def across(n):
        pairs = [
            (block, held.at[z, d]),
            (meta, metas.at[z, d]),
            (gate.at[1 - d], all_gate.at[d]),
            (up.at[1 - d], all_up.at[d]),
        ] + [
            (down.at[1 - d, :, pl.ds(j * span, span)], all_down.at[j, d]) for j in range(chunks)
        ]
        return remote(*pairs[n], y_send.at[n], y_recv.at[n], e, 1 - d)

    def own(n):
        pairs = [
            (block, held.at[z, d]),
            (meta, metas.at[z, d]),
            (gate.at[d], all_gate.at[d]),
            (up.at[d], all_up.at[d]),
        ] + [(down.at[d, :, pl.ds(j * span, span)], all_down.at[j, d]) for j in range(chunks)]
        src, dst = pairs[n]
        return pltpu.make_async_copy(src, dst, o_sem.at[n])

    for n in range(4 + chunks):
        across(n).start()
    for n in range(2):
        own(n).start()
    for n in range(2):
        own(n).wait()

    def along(way, at, dd):
        to = e + 4 if way else e - 4
        return [
            remote(
                held.at[at, dd], held.at[at, dd],
                z_send.at[way, at, dd, 0], z_recv.at[at, dd, 0], to, d,
            ),
            remote(
                metas.at[at, dd], metas.at[at, dd],
                z_send.at[way, at, dd, 1], z_recv.at[at, dd, 1], to, d,
            ),
        ]

    def sideways(at, dd, n):
        return [
            remote(
                chosen.at[n, offset - 1],
                taken.at[offset, at, dd],
                x_send.at[n, offset - 1],
                x_recv.at[at, dd, offset - 1],
                beside(e, offset),
                d,
            )
            for offset in range(1, 4)
        ]

    def swaps(kind, part):
        src = [gate, up, down][kind]
        dst = [got_gate, got_up, got_down][kind]
        size = src.shape[1] // blocks
        lot = pl.ds(pl.multiple_of(part * size, size), size)
        return [
            (
                remote(
                    src.at[0, lot], dst.at[bit, lot],
                    s_send.at[kind, part, n], s_recv.at[kind, part, n],
                    flip(e, 1 << bit), d,
                ),
                cores,
            )
            for n, (bit, cores) in enumerate(moves)
        ]

    def swap_start(kind, part):
        for copy, cores in swaps(kind, part):
            for_cores(cores, c, copy.start)

    upper = (
        lax.broadcasted_iota(jnp.int32, (lanes, lanes), 0)
        < lax.broadcasted_iota(jnp.int32, (lanes, lanes), 1)
    ).astype(F32).astype(BF16)
    slots = lax.broadcasted_iota(jnp.int32, (cap, lanes), 0).astype(F32)
    places = lax.broadcasted_iota(jnp.int32, (8, lanes), 0)

    def place(rank):
        at = jnp.int32(0)
        for k in range(lines):
            at = at + (1 - jnp.minimum(jnp.abs(rank - k), 1)) * pick(
                [order[p][k] for p in range(lines)], z
            )
        return at

    def spread(n, _):
        at, dd = place(n // 2), (d + n % 2) % 2

        @pl.when(n == 1)
        def _():
            across(0).wait_recv()
            across(1).wait_recv()

        @pl.when(n > 1)
        def _():
            for copy in along(1, at, dd):
                copy.wait_recv()

        @pl.when(jnp.logical_and(at <= z, z < lines - 1))
        def _():
            for copy in along(1, at, dd):
                copy.start()

        @pl.when(jnp.logical_and(at >= z, z > 0))
        def _():
            for copy in along(0, at, dd):
                copy.start()

        tags = metas[at, dd].astype(F32)
        ids, parts = tags[:top], tags[top:]
        member = jnp.zeros((8, lanes), F32)
        factors = []
        for offset in range(4):
            expert = (2 * beside(e, offset) + d).astype(F32)
            same = ids == expert
            row = jnp.max(jnp.where(same, 1.0, 0.0), axis=0, keepdims=True)
            factors.append(jnp.sum(jnp.where(same, parts, 0.0), axis=0, keepdims=True))
            member = jnp.where(places == offset, row, member)
        rank = jnp.dot(member.astype(BF16), upper, preferred_element_type=F32)
        hits, mixes = [], []
        for offset in range(4):
            hit = jnp.logical_and(
                rank[offset : offset + 1] == slots, member[offset : offset + 1] > 0.5
            )
            hits.append(jnp.where(hit, 1.0, 0.0))
            mixes.append(jnp.where(hit, factors[offset], 0.0))
        hit = jnp.concatenate(hits, axis=0).astype(BF16)[:, :rows]
        mats[at, dd] = jnp.transpose(jnp.concatenate(mixes, axis=0)).astype(BF16)

        def columns(j, _):
            cols = pl.ds(pl.multiple_of(j * span, span), span)
            picked = jnp.dot(
                hit, held[at, dd, :, cols], preferred_element_type=F32
            ).astype(BF16)
            taken[0, at, dd, :, cols] = picked[:cap]
            for offset in range(1, 4):
                chosen[n, offset - 1, :, cols] = picked[offset * cap : (offset + 1) * cap]
            return 0

        lax.fori_loop(0, chunks, columns, 0)
        for copy in sideways(at, dd, n):
            copy.start()
        swap_start(0, n)
        return 0

    lax.fori_loop(0, blocks, spread, 0)
    for n in range(2, 4 + chunks):
        own(n).start()

    def settle(n, _):
        at, dd = place(n // 2), (d + n % 2) % 2

        @pl.when(jnp.logical_and(at <= z, z < lines - 1))
        def _():
            for copy in along(1, at, dd):
                copy.wait_send()

        @pl.when(jnp.logical_and(at >= z, z > 0))
        def _():
            for copy in along(0, at, dd):
                copy.wait_send()

        for copy in sideways(at, dd, n):
            copy.wait()
        swap_start(1, n)
        return 0

    lax.fori_loop(0, blocks, settle, 0)
    lot = blocks * cap

    def product(offset, weight):
        return jnp.dot(
            taken[offset].reshape(lot, width),
            weight[...].reshape(width, weight.shape[-1]),
            preferred_element_type=F32,
        )

    def activate(offset, _):
        gates[offset] = product(offset, all_gate)
        return 0

    own(2).wait()
    across(2).wait()
    lax.fori_loop(0, 4, activate, 0)

    def combine(offset, _):
        act = gates[offset]
        act = act / (1.0 + jnp.exp(-act))
        hidden[offset] = (act * product(offset, all_up)).astype(BF16)
        return 0

    own(3).wait()
    across(3).wait()
    lax.fori_loop(0, 4, combine, 0)
    for n in range(4, 4 + chunks):
        own(n).wait()

    def distant(k):
        return place(lines - 1 - k)

    def local(j, at):
        return pltpu.make_async_copy(outs.at[j, 0, at], back.at[j, at, :, 0], b_sem.at[j, at])

    def homeward(j, at):
        return [
            remote(
                outs.at[j, offset, at],
                back.at[j, at, :, offset],
                b_send.at[j, at, offset - 1],
                b_recv.at[j, at, offset - 1],
                beside(e, offset),
                d,
            )
            for offset in range(1, 4)
        ]

    def reduced(way, j, at):
        to = e + 4 if way else e - 4
        land = from_left if way else from_right
        return remote(
            sums.at[j, at], land.at[j, at], r_send.at[j, at], r_recv.at[way, j, at], to, d
        )

    def exchanged(j):
        return remote(
            sums.at[j, z, 1 - d], other.at[j], m_send.at[j], m_recv.at[j], e, 1 - d
        )

    def produce(j):
        for n in range(chunks):

            @pl.when(j == n)
            def _():
                across(4 + n).wait()

        def one(offset, _):
            out = jnp.dot(
                hidden[offset],
                all_down[j].reshape(hidden.shape[-1], span),
                preferred_element_type=F32,
            )
            outs[j, offset] = out.astype(BF16).reshape(lines, 2, cap, span)
            return 0

        lax.fori_loop(0, 4, one, 0)

        def send(k, _):
            at = distant(k)
            local(j, at).start()
            for copy in homeward(j, at):
                copy.start()
            return 0

        lax.fori_loop(0, lines, send, 0)

    def reduce(j):
        def one(k, _):
            at = distant(k)
            local(j, at).wait()
            for copy in homeward(j, at):
                copy.wait()
            for dd in range(2):
                total[dd] = jnp.dot(
                    mats[at, dd][:rows],
                    back[j, at, dd].reshape(4 * cap, span),
                    preferred_element_type=F32,
                )

            @pl.when(jnp.logical_and(at >= z, z > 0))
            def _():
                reduced(1, j, at).wait_recv()
                total[...] += from_left[j, at].astype(F32)

            @pl.when(jnp.logical_and(at <= z, z < lines - 1))
            def _():
                reduced(0, j, at).wait_recv()
                total[...] += from_right[j, at].astype(F32)

            sums[j, at] = total[...].astype(BF16)

            @pl.when(at > z)
            def _():
                reduced(1, j, at).start()

            @pl.when(at < z)
            def _():
                reduced(0, j, at).start()

            return 0

        lax.fori_loop(0, lines, one, 0)
        exchanged(j).start()

    def turn(i, _):
        @pl.when(i < chunks)
        def _():
            produce(i)
            for n in range(blocks // chunks):
                swap_start(2, i * (blocks // chunks) + n)

        @pl.when(i > 0)
        def _():
            reduce(i - 1)

        return 0

    lax.fori_loop(0, chunks + 1, turn, 0)

    def close(j, _):
        exchanged(j).wait()
        cols = pl.ds(pl.multiple_of(j * span, span), span)
        mixed[:, cols] = (sums[j, z, d].astype(F32) + other[j].astype(F32)).astype(BF16)

        def sent(k, _):
            at = distant(k)

            @pl.when(at > z)
            def _():
                reduced(1, j, at).wait_send()

            @pl.when(at < z)
            def _():
                reduced(0, j, at).wait_send()

            return 0

        lax.fori_loop(0, lines, sent, 0)
        return 0

    lax.fori_loop(0, chunks, close, 0)
    across(0).wait_send()
    across(1).wait_send()

    def swapped(n, _):
        for kind in range(3):
            for copy, cores in swaps(kind, n):
                for_cores(cores, c, copy.wait)
        return 0

    lax.fori_loop(0, blocks, swapped, 0)


def layer(lines, cap, moves, key, bits, block, meta, gate, up, down):
    rows, width = block.shape
    lanes = meta.shape[1]
    blocks = 2 * lines
    half, inner = gate.shape[1:]
    chunks = 4
    span = width // chunks
    part = (chunks, lines, 2, rows, span)
    sem = pltpu.SemaphoreType.DMA
    return pl.pallas_call(
        functools.partial(layer_kernel, lines, cap, chunks, moves),
        name="layer",
        out_shape=(
            jax.ShapeDtypeStruct((rows, width), BF16),
            jax.ShapeDtypeStruct((bits, half, inner), BF16),
            jax.ShapeDtypeStruct((bits, half, inner), BF16),
            jax.ShapeDtypeStruct((bits,) + down.shape[1:], BF16),
        ),
        in_specs=[INV, INV, ANY, ANY, ANY],
        out_specs=(INV, ANY, ANY, ANY),
        scratch_shapes=[
            pltpu.VMEM((lines, 2, rows, width), BF16),
            pltpu.VMEM((lines, 2, meta.shape[0], lanes), BF16),
            pltpu.VMEM((blocks, 3, cap, width), BF16),
            pltpu.VMEM((4, lines, 2, cap, width), BF16),
            pltpu.VMEM((lines, 2, lanes, 4 * cap), BF16),
            pltpu.VMEM((2, half, inner), BF16),
            pltpu.VMEM((2, half, inner), BF16),
            pltpu.VMEM((chunks, 2, down.shape[1], span), BF16),
            pltpu.VMEM((4, blocks * cap, inner), F32),
            pltpu.VMEM((4, blocks * cap, inner), BF16),
            pltpu.VMEM((chunks, 4, lines, 2, cap, span), BF16),
            pltpu.VMEM((chunks, lines, 2, 4, cap, span), BF16),
            pltpu.VMEM(part, BF16),
            pltpu.VMEM(part, BF16),
            pltpu.VMEM(part, BF16),
            pltpu.VMEM((2, rows, span), F32),
            pltpu.VMEM((chunks, rows, span), BF16),
            sem((4 + chunks,)),
            sem((4 + chunks,)),
            sem((4 + chunks,)),
            sem((2, lines, 2, 2)),
            sem((lines, 2, 2)),
            sem((blocks, 3)),
            sem((lines, 2, 3)),
            sem((chunks, lines)),
            sem((chunks, lines, 3)),
            sem((chunks, lines, 3)),
            sem((chunks, lines)),
            sem((2, chunks, lines)),
            sem((chunks,)),
            sem((chunks,)),
            sem((3, blocks, len(moves))),
            sem((3, blocks, len(moves))),
        ],
        compiler_params=pltpu.CompilerParams(
            collective_id=key, has_side_effects=True, vmem_limit_bytes=60 << 20
        ),
    )(block, meta, gate, up, down)


def square_body(
    tokens, norm_gain, expert_ids, route_weights, gate_weight, up_weight, down_weight, pair_list
):
    count = lax.axis_size("expert")
    dp = lax.axis_size("dp")
    e, d = lax.axis_index("expert"), lax.axis_index("dp")
    per_device = gate_weight.shape[0]
    rows, top = expert_ids.shape
    width = tokens.shape[1]
    lines = count // 4
    cap = 4 * rows * top // (3 * count * per_device)
    bits = count.bit_length() - 1
    lanes = -(-rows // 128) * 128

    values = tokens.astype(F32)
    scale = lax.rsqrt(jnp.mean(values * values, axis=-1, keepdims=True) + 1e-06)
    normed = (values * scale * norm_gain).astype(BF16)
    meta = jnp.concatenate([expert_ids.astype(BF16), route_weights.astype(BF16)], axis=1)
    meta = jnp.pad(meta.T, ((0, 0), (0, lanes - rows)), constant_values=-1)

    places = jnp.arange(count, dtype=jnp.int32)
    distances = jnp.bitwise_xor(pair_list, places)
    choice = jnp.int32(0)
    for n, bit in enumerate(range(1, bits)):
        choice = choice + (jnp.any(distances == (1 << bit)).astype(jnp.int32) << n)
    move_sets = []
    for mask in range(1 << (bits - 1)):
        move_sets.append(
            [(0, (0, 1))] + [(n + 1, (0, 1)) for n in range(bits - 1) if mask >> n & 1]
        )

    def run(moves, key):
        return lambda *args: layer(lines, cap, moves, key, bits, *args)

    mixed, got_gate, got_up, got_down = lax.switch(
        choice,
        [run(moves, key) for key, moves in enumerate(move_sets)],
        normed, meta, gate_weight, up_weight, down_weight,
    )
    distance = jnp.bitwise_xor(pair_list[e], e)
    slot = jnp.int32(0)
    for bit in range(1, bits):
        slot = slot + jnp.where(distance >= (1 << bit), 1, 0)

    def held(own, got):
        return jnp.where(distance == 0, own[:1], lax.dynamic_slice_in_dim(got, slot, 1, 0))

    return (
        mixed,
        held(gate_weight, got_gate),
        held(up_weight, got_up),
        held(down_weight, got_down),
    )


def body(*args):
    dp, count = lax.axis_size("dp"), lax.axis_size("expert")
    per_device = args[4].shape[0]
    rows, top = args[2].shape
    square = dp == 2 and per_device == 2 and count % 4 == 0 and rows * top % (3 * count) == 0
    return square_body(*args) if square else wide_body(*args)


def solution(mesh):
    in_specs = (
        P(("expert", "dp"), None),
        P(),
        P(("expert", "dp"), None),
        P(("expert", "dp"), None),
        P("expert", "dp", None),
        P("expert", "dp", None),
        P("expert", "dp", None),
        P(),
    )
    out_specs = (
        P(("expert", "dp"), None),
        P("expert", "dp", None),
        P("expert", "dp", None),
        P("expert", "dp", None),
    )
    return jax.shard_map(body, mesh=mesh, in_specs=in_specs, out_specs=out_specs, check_vma=False)
```

```python
import functools
import itertools

import jax
import jax.numpy as jnp
from jax import lax
from jax.experimental import pallas as pl
from jax.experimental.pallas import tpu as pltpu
from jax.sharding import PartitionSpec as P

F32 = jnp.float32
BF16 = jnp.bfloat16
MESH = pl.DeviceIdType.MESH
ANY = pl.BlockSpec(memory_space=pl.ANY)
INV = pl.BlockSpec(memory_space=pltpu.VMEM)


def bit_route(count, bit, cores):
    return [
        (e, e ^ (1 << bit)) for e in range(count) if e ^ (1 << bit) < count and (e & 1) in cores
    ]


def swap_branch(moves, count):
    def run(blocks, base, distance):
        arrived = [
            [lax.ppermute(b, "expert", bit_route(count, bit, cores)) for b in blocks]
            for bit, cores in moves
        ]
        out = base
        for (bit, _), got in zip(moves, arrived):
            out = [jnp.where(distance == (1 << bit), a, o) for a, o in zip(got, out)]
        return tuple(out)

    return run


def swap(blocks, base, pair_list, count, always, bits):
    mine = lax.axis_index("expert")
    places = jnp.arange(count, dtype=jnp.int32)
    distances = jnp.bitwise_xor(pair_list, places)
    distance = jnp.bitwise_xor(pair_list[mine], mine)
    choice = jnp.int32(0)
    for n, bit in enumerate(bits):
        for core in range(2):
            used = jnp.any((distances == (1 << bit)) & (places & 1 == core)).astype(jnp.int32)
            choice = choice + (used << (2 * n + core))
    branches = []
    for mask in range(1 << (2 * len(bits))):
        moves = [(bit, (0, 1)) for bit in always]
        for n, bit in enumerate(bits):
            cores = tuple(c for c in range(2) if mask >> (2 * n + c) & 1)
            if cores:
                moves.append((bit, cores))
        branches.append(swap_branch(moves, count))
    return list(lax.switch(choice, branches, list(blocks), list(base), distance))


def placing_of(ids, parity, count, per_device, capacity):
    rows = ids.shape[0]
    experts = jnp.arange(count, dtype=jnp.int32) * per_device + parity
    equal = ids[:, :, None] == experts[None, None, :]
    member = jnp.any(equal, axis=1)
    lower = jnp.tril(jnp.ones((rows, rows), BF16), -1)
    rank = jnp.dot(lower, member.astype(BF16), preferred_element_type=F32).astype(jnp.int32)
    rank = jnp.where(member, rank, -1)
    slots = jnp.arange(capacity, dtype=jnp.int32)
    hit = rank.T[:, None, :] == slots[None, :, None]
    return equal, hit


def wide_body(
    tokens, norm_gain, expert_ids, route_weights, gate_weight, up_weight, down_weight, pair_list
):
    count = lax.axis_size("expert")
    dp = lax.axis_size("dp")
    per_device = gate_weight.shape[0]
    group = per_device if dp % per_device == 0 else 1
    experts_all = count * per_device
    rows, top = expert_ids.shape
    width = tokens.shape[1]
    capacity = max(2, 4 * rows * top // (3 * experts_all))
    d = lax.axis_index("dp")
    parity = d % group

    values = tokens.astype(F32)
    scale = lax.rsqrt(jnp.mean(values * values, axis=-1, keepdims=True) + 1e-06)
    normed = (values * scale * norm_gain).astype(BF16)
    route_bf = route_weights.astype(BF16)

    def in_group(block, shift):
        if shift % group == 0:
            return block
        route = [(i, i // group * group + (i % group + shift) % group) for i in range(dp)]
        return lax.ppermute(block, "dp", route)

    token_sets = [
        (in_group(normed, s), in_group(expert_ids, s), in_group(route_bf, s)) for s in range(group)
    ]
    token_sets, weights = lax.optimization_barrier(
        (token_sets, (gate_weight, up_weight, down_weight))
    )

    def shards(weight):
        out = []
        for s in range(dp):
            sent = lax.dynamic_index_in_dim(weight, (d + s) % group, 0, keepdims=False)
            if s:
                sent = lax.ppermute(sent, "dp", [(i, (i + s) % dp) for i in range(dp)])
            out.append(sent)
        return out

    gates, ups, downs = [shards(w) for w in weights]

    outgoing, weightings = [], []
    for normed_s, ids_s, route_s in token_sets:
        equal, hit = placing_of(ids_s, parity, count, per_device, capacity)
        picked = jnp.dot(
            hit.reshape(count * capacity, rows).astype(BF16), normed_s, preferred_element_type=F32
        ).astype(BF16)
        outgoing.append(picked.reshape(count, capacity, width))
        factor = jnp.sum(jnp.where(equal, route_s[:, :, None], jnp.zeros((), BF16)), axis=1)
        weightings.append(
            jnp.where(hit, factor.T[:, None, :], jnp.zeros((), BF16)).reshape(
                count * capacity, rows
            )
        )
    outgoing = jnp.concatenate(outgoing, axis=1)
    bit_total = count.bit_length() - 1
    firsts = [gate_weight[0], up_weight[0], down_weight[0]]
    early = list(range(1, min(3, bit_total)))
    late = list(range(3, bit_total))
    outgoing, pairs = lax.optimization_barrier((outgoing, pair_list))
    received = lax.all_to_all(outgoing, "expert", split_axis=0, concat_axis=0, tiled=True)
    half_held = swap(firsts, firsts, pairs, count, [], early)
    received, half_held = lax.optimization_barrier((received, half_held))
    columns = received.reshape(count * group * capacity, width)

    def times(x, parts):
        size = parts[0].shape[0]
        total = None
        for s, part in enumerate(parts):
            at = (d - s) % dp
            piece = lax.dynamic_slice_in_dim(x, at * size, size, axis=1)
            term = jnp.dot(piece, part, preferred_element_type=F32)
            total = term if total is None else total + term
        return total

    hidden = (jax.nn.silu(times(columns, gates)) * times(columns, ups)).astype(BF16)
    expert_out = times(hidden, downs).astype(BF16)
    expert_out, pairs = lax.optimization_barrier((expert_out, pairs))
    held = swap(firsts, half_held, pairs, count, [0], late)
    returned = lax.all_to_all(
        expert_out.reshape(count, group * capacity, width),
        "expert",
        split_axis=0,
        concat_axis=0,
        tiled=True,
    )
    returned, held = lax.optimization_barrier((returned, held))
    total = None
    for s in range(group):
        part = returned[:, s * capacity : (s + 1) * capacity].reshape(count * capacity, width)
        mix = jnp.einsum("sr,sd->rd", weightings[s], part, preferred_element_type=F32)
        if s:
            mix = in_group(mix.astype(BF16), group - s).astype(F32)
        total = mix if total is None else total + mix
    return (total.astype(BF16), held[0][None], held[1][None], held[2][None])


def flip(index, step):
    return index + step * (1 - 2 * ((index // step) % 2))


def pick(table, index):
    value = jnp.int32(table[0])
    for n in range(1, len(table)):
        value = value + jnp.int32(table[n] - table[0]) * (1 - jnp.minimum(jnp.abs(index - n), 1))
    return value


def near_first(places):
    return [sorted(range(places), key=lambda p: (abs(p - at), p)) for at in range(places)]


def greet(lines, z, e, d, moves):
    barrier = pltpu.get_barrier_semaphore()

    def signal(to_e, to_d):
        pl.semaphore_signal(barrier, inc=1, device_id=(to_e, to_d), device_id_type=MESH)

    signal(e, 1 - d)
    for offset in range(1, 4):
        signal(beside(e, offset), d)
    total = 4 + jnp.minimum(z, 1) + jnp.minimum(lines - 1 - z, 1)

    @pl.when(z > 0)
    def _():
        signal(e - 4, d)

    @pl.when(z < lines - 1)
    def _():
        signal(e + 4, d)

    for bit, _ in moves:
        if bit > 2:
            signal(flip(e, 1 << bit), d)
            total = total + 1
    pl.semaphore_wait(barrier, total)


def beside(e, offset):
    for bit in range(2):
        if offset >> bit & 1:
            e = flip(e, 1 << bit)
    return e


def remote(src, dst, send, recv, to_e, to_d):
    return pltpu.make_async_remote_copy(
        src_ref=src,
        dst_ref=dst,
        send_sem=send,
        recv_sem=recv,
        device_id=(to_e, to_d),
        device_id_type=MESH,
    )


def for_cores(cores, c, act):
    if len(cores) == 2:
        act()
    else:
        pl.when(c == cores[0])(act)


def layer_kernel(
    lines, cap, chunks, moves, block, meta, gate, up, down,
    mixed, got_gate, got_up, got_down,
    held, metas, chosen, taken, mats, inward, all_down, gates, hidden,
    outs, back, sums, from_left, from_right, total, other,
    o_sem, y_send, y_recv, z_send, z_recv, x_send, x_recv,
    b_sem, b_send, b_recv, r_send, r_recv, m_send, m_recv, s_send, s_recv,
):
    e, d = lax.axis_index("expert"), lax.axis_index("dp")
    z, c = e // 4, e % 2
    rows, width = block.shape
    lanes = meta.shape[1]
    top = meta.shape[0] // 2
    blocks = 2 * lines
    span = width // chunks
    tile = span
    order = near_first(lines)
    greet(lines, z, e, d, moves)

    def across(n):
        pairs = [
            (block, held.at[z, d]),
            (meta, metas.at[z, d]),
            (gate.at[1 - d], inward.at[0, d]),
            (up.at[1 - d], inward.at[1, d]),
        ] + [
            (down.at[1 - d, :, pl.ds(j * span, span)], all_down.at[j, d]) for j in range(chunks)
        ]
        return remote(*pairs[n], y_send.at[n], y_recv.at[n], e, 1 - d)

    def own(n):
        pairs = [
            (block, held.at[z, d]),
            (meta, metas.at[z, d]),
            (gate.at[d], inward.at[0, d]),
            (up.at[d], inward.at[1, d]),
        ] + [(down.at[d, :, pl.ds(j * span, span)], all_down.at[j, d]) for j in range(chunks)]
        src, dst = pairs[n]
        return pltpu.make_async_copy(src, dst, o_sem.at[n])

    for n in range(4 + chunks):
        across(n).start()
    for n in range(2):
        own(n).start()
    for n in range(2):
        own(n).wait()

    def further(at, centre):
        return at + (lines - at) * (1 - jnp.minimum(jnp.abs(at - centre), 1))

    def along(way, at, dd):
        to = e + 4 if way else e - 4
        slot = at if way else further(at, z)
        return [
            remote(
                ref.at[at, dd], ref.at[at, dd],
                z_send.at[slot, dd, n], z_recv.at[at, dd, n], to, d,
            )
            for n, ref in enumerate([held, metas])
        ]

    def sideways(at, dd, n):
        return [
            remote(
                chosen.at[n, offset - 1],
                taken.at[offset, at, dd],
                x_send,
                x_recv,
                beside(e, offset),
                d,
            )
            for offset in range(1, 4)
        ]

    def swaps(kind, part):
        src = [gate, up, down][kind]
        dst = [got_gate, got_up, got_down][kind]
        size = src.shape[1] // blocks
        lot = pl.ds(pl.multiple_of(part * size, size), size)
        return [
            (
                remote(
                    src.at[0, lot], dst.at[bit, lot],
                    s_send.at[kind, n], s_recv.at[kind, n],
                    flip(e, 1 << bit), d,
                ),
                cores,
            )
            for n, (bit, cores) in enumerate(moves)
        ]

    def swap_start(kind, part):
        for copy, cores in swaps(kind, part):
            for_cores(cores, c, copy.start)

    upper = (
        lax.broadcasted_iota(jnp.int32, (lanes, lanes), 0)
        < lax.broadcasted_iota(jnp.int32, (lanes, lanes), 1)
    ).astype(F32).astype(BF16)
    slots = lax.broadcasted_iota(jnp.int32, (cap, lanes), 0).astype(F32)
    places = lax.broadcasted_iota(jnp.int32, (8, lanes), 0)

    def place(rank):
        at = jnp.int32(0)
        for k in range(lines):
            at = at + (1 - jnp.minimum(jnp.abs(rank - k), 1)) * pick(
                [order[p][k] for p in range(lines)], z
            )
        return at

    def spread(n, _):
        at, dd = place(n // 2), (d + n % 2) % 2

        @pl.when(n == 1)
        def _():
            across(0).wait_recv()
            across(1).wait_recv()

        @pl.when(n > 1)
        def _():
            for copy in along(1, at, dd):
                copy.wait_recv()

        @pl.when(jnp.logical_and(at <= z, z < lines - 1))
        def _():
            for copy in along(1, at, dd):
                copy.start()

        @pl.when(jnp.logical_and(at >= z, z > 0))
        def _():
            for copy in along(0, at, dd):
                copy.start()

        tags = metas[at, dd].astype(F32)
        ids, parts = tags[:top], tags[top:]
        member = jnp.zeros((8, lanes), F32)
        factors = []
        for offset in range(4):
            expert = (2 * beside(e, offset) + d).astype(F32)
            same = ids == expert
            row = jnp.max(jnp.where(same, 1.0, 0.0), axis=0, keepdims=True)
            factors.append(jnp.sum(jnp.where(same, parts, 0.0), axis=0, keepdims=True))
            member = jnp.where(places == offset, row, member)
        rank = jnp.dot(member.astype(BF16), upper, preferred_element_type=F32)
        hits, mixes = [], []
        for offset in range(4):
            hit = jnp.logical_and(
                rank[offset : offset + 1] == slots, member[offset : offset + 1] > 0.5
            )
            hits.append(jnp.where(hit, 1.0, 0.0))
            mixes.append(jnp.where(hit, factors[offset], 0.0))
        hit = jnp.concatenate(hits, axis=0).astype(BF16)[:, :rows]
        mats[at, dd] = jnp.transpose(jnp.concatenate(mixes, axis=0)).astype(BF16)

        def columns(j, _):
            cols = pl.ds(pl.multiple_of(j * tile, tile), tile)
            picked = jnp.dot(
                hit, held[at, dd, :, cols], preferred_element_type=F32
            ).astype(BF16)
            taken[0, at, dd, :, cols] = picked[:cap]
            for offset in range(1, 4):
                chosen[n, offset - 1, :, cols] = picked[offset * cap : (offset + 1) * cap]
            return 0

        lax.fori_loop(0, width // tile, columns, 0)
        for copy in sideways(at, dd, n):
            copy.start()
        swap_start(0, n)
        return 0

    lax.fori_loop(0, blocks, spread, 0)
    for n in range(2, 4 + chunks):
        own(n).start()

    def settle(n, _):
        at, dd = place(n // 2), (d + n % 2) % 2

        @pl.when(jnp.logical_and(at <= z, z < lines - 1))
        def _():
            for copy in along(1, at, dd):
                copy.wait_send()

        @pl.when(jnp.logical_and(at >= z, z > 0))
        def _():
            for copy in along(0, at, dd):
                copy.wait_send()

        swap_start(1, n)
        return 0

    lax.fori_loop(0, blocks, settle, 0)
    remote(chosen, chosen, x_send, x_recv, e, 1 - d).wait_send()
    rest = taken.at[pl.ds(1, 3)]
    remote(rest, rest, x_send, x_recv, e, 1 - d).wait_recv()
    lot = blocks * cap

    inner = hidden.shape[-1]
    wide = inner
    tiles = inner // wide

    def project(kind, _):
        for n in range(2):

            @pl.when(kind == n)
            def _():
                own(2 + n).wait()
                across(2 + n).wait()

        def one(i, _):
            offset = i // tiles
            cols = pl.ds(pl.multiple_of(i % tiles * wide, wide), wide)
            value = jnp.dot(
                taken[offset].reshape(lot, width),
                inward[kind, :, :, cols].reshape(width, wide),
                preferred_element_type=F32,
            )

            @pl.when(kind == 0)
            def _():
                gates[offset, :, cols] = value / (1.0 + jnp.exp(-value))

            @pl.when(kind == 1)
            def _():
                hidden[offset, :, cols] = (gates[offset, :, cols] * value).astype(BF16)

            return 0

        return lax.fori_loop(0, 4 * tiles, one, 0)

    lax.fori_loop(0, 2, project, 0)
    for n in range(4, 4 + chunks):
        own(n).wait()

    def distant(k):
        return place(lines - 1 - k)

    def local(j):
        return pltpu.make_async_copy(outs.at[j, 0], back.at[j, :, :, 0], b_sem.at[j])

    def homeward(j, at):
        return [
            remote(
                outs.at[j, offset, at],
                back.at[j, at, :, offset],
                b_send.at[j],
                b_recv.at[j, at],
                beside(e, offset),
                d,
            )
            for offset in range(1, 4)
        ]

    def reduced(way, j, at, here):
        to = e + 4 if way else e - 4
        land = from_left if way else from_right
        slot = at if way else further(at, here)
        return remote(
            sums.at[j, at], land.at[j, at], r_send.at[j], r_recv.at[j, slot], to, d
        )

    def exchanged(j):
        return remote(
            sums.at[j, z, 1 - d], other.at[j], m_send.at[j], m_recv.at[j], e, 1 - d
        )

    def produce(j):
        for n in range(chunks):

            @pl.when(j == n)
            def _():
                across(4 + n).wait()

        def one(i, _):
            offset = i // (span // tile)
            cols = pl.ds(pl.multiple_of(i % (span // tile) * tile, tile), tile)
            out = jnp.dot(
                hidden[offset],
                all_down[j, :, :, cols].reshape(inner, tile),
                preferred_element_type=F32,
            )
            outs[j, offset, :, :, :, cols] = out.astype(BF16).reshape(lines, 2, cap, tile)
            return 0

        lax.fori_loop(0, 4 * (span // tile), one, 0)
        local(j).start()

        def send(k, _):
            at = distant(k)
            for copy in homeward(j, at):
                copy.start()
            return 0

        lax.fori_loop(0, lines, send, 0)

    def reduce(i):
        @pl.when(jnp.logical_and(i > 0, i < chunks + 1))
        def _():
            local(i - 1).wait()

        def one(k, _):
            j = i - 1 - k // (lines // 2)

            @pl.when(jnp.logical_and(j >= 0, j < chunks))
            def _():
                step(j, k)

            return 0

        def step(j, k):
            at = distant(k)
            come = back.at[j, at, :, pl.ds(1, 3)]
            remote(come, come, b_send.at[j], b_recv.at[j, at], e, 1 - d).wait_recv()
            left = jnp.logical_and(at >= z, z > 0)
            right = jnp.logical_and(at <= z, z < lines - 1)

            @pl.when(left)
            def _():
                reduced(1, j, at, z).wait_recv()

            @pl.when(right)
            def _():
                reduced(0, j, at, z).wait_recv()

            def piece(i, _):
                dd = i // (span // tile)
                cols = pl.ds(pl.multiple_of(i % (span // tile) * tile, tile), tile)
                total[...] = jnp.dot(
                    mats[at, dd, :rows],
                    back[j, at, dd, :, :, cols].reshape(4 * cap, tile),
                    preferred_element_type=F32,
                )

                @pl.when(left)
                def _():
                    total[...] += from_left[j, at, dd, :, cols].astype(F32)

                @pl.when(right)
                def _():
                    total[...] += from_right[j, at, dd, :, cols].astype(F32)

                sums[j, at, dd, :, cols] = total[...].astype(BF16)
                return 0

            lax.fori_loop(0, 2 * (span // tile), piece, 0)

            @pl.when(at > z)
            def _():
                reduced(1, j, at, z).start()

            @pl.when(at < z)
            def _():
                reduced(0, j, at, z - 1).start()

            @pl.when(k == lines - 1)
            def _():
                exchanged(j).start()

        lax.fori_loop(0, lines, one, 0)

    def turn(i, _):
        @pl.when(i < chunks)
        def _():
            produce(i)
            for n in range(blocks // chunks):
                swap_start(2, i * (blocks // chunks) + n)

        reduce(i)
        return 0

    lax.fori_loop(0, chunks + 2, turn, 0)

    def close(j, _):
        exchanged(j).wait()
        cols = pl.ds(pl.multiple_of(j * span, span), span)
        mixed[:, cols] = (sums[j, z, d].astype(F32) + other[j].astype(F32)).astype(BF16)

        gone = sums.at[j, pl.ds(0, lines - 1)]
        remote(gone, gone, r_send.at[j], m_recv.at[j], e, 1 - d).wait_send()
        gone = outs.at[j, pl.ds(1, 3)]
        remote(gone, gone, b_send.at[j], m_recv.at[j], e, 1 - d).wait_send()
        return 0

    lax.fori_loop(0, chunks, close, 0)
    across(0).wait_send()
    across(1).wait_send()

    for kind, (src, dst) in enumerate([(gate, got_gate), (up, got_up), (down, got_down)]):
        for n, (bit, cores) in enumerate(moves):
            copy = remote(
                src.at[0], dst.at[bit], s_send.at[kind, n], s_recv.at[kind, n], e, 1 - d
            )
            for_cores(cores, c, copy.wait)


def layer(lines, cap, moves, key, bits, block, meta, gate, up, down):
    rows, width = block.shape
    lanes = meta.shape[1]
    blocks = 2 * lines
    half, inner = gate.shape[1:]
    chunks = 4
    span = width // chunks
    tile = span
    part = (chunks, lines, 2, rows, span)
    sem = pltpu.SemaphoreType.DMA
    return pl.pallas_call(
        functools.partial(layer_kernel, lines, cap, chunks, moves),
        name="layer",
        out_shape=(
            jax.ShapeDtypeStruct((rows, width), BF16),
            jax.ShapeDtypeStruct((bits, half, inner), BF16),
            jax.ShapeDtypeStruct((bits, half, inner), BF16),
            jax.ShapeDtypeStruct((bits,) + down.shape[1:], BF16),
        ),
        in_specs=[INV, INV, ANY, ANY, ANY],
        out_specs=(INV, ANY, ANY, ANY),
        scratch_shapes=[
            pltpu.VMEM((lines, 2, rows, width), BF16),
            pltpu.VMEM((lines, 2, meta.shape[0], lanes), BF16),
            pltpu.VMEM((blocks, 3, cap, width), BF16),
            pltpu.VMEM((4, lines, 2, cap, width), BF16),
            pltpu.VMEM((lines, 2, lanes, 4 * cap), BF16),
            pltpu.VMEM((2, 2, half, inner), BF16),
            pltpu.VMEM((chunks, 2, down.shape[1], span), BF16),
            pltpu.VMEM((4, blocks * cap, inner), F32),
            pltpu.VMEM((4, blocks * cap, inner), BF16),
            pltpu.VMEM((chunks, 4, lines, 2, cap, span), BF16),
            pltpu.VMEM((chunks, lines, 2, 4, cap, span), BF16),
            pltpu.VMEM(part, BF16),
            pltpu.VMEM(part, BF16),
            pltpu.VMEM(part, BF16),
            pltpu.VMEM((rows, tile), F32),
            pltpu.VMEM((chunks, rows, span), BF16),
            sem((4 + chunks,)),
            sem((4 + chunks,)),
            sem((4 + chunks,)),
            sem((lines + 1, 2, 2)),
            sem((lines, 2, 2)),
            sem,
            sem,
            sem((chunks,)),
            sem((chunks,)),
            sem((chunks, lines)),
            sem((chunks,)),
            sem((chunks, lines + 1)),
            sem((chunks,)),
            sem((chunks,)),
            sem((3, len(moves))),
            sem((3, len(moves))),
        ],
        compiler_params=pltpu.CompilerParams(
            collective_id=key, has_side_effects=True, vmem_limit_bytes=60 << 20
        ),
    )(block, meta, gate, up, down)


def distant_kernel(classes, gate, up, down, far_gate, far_up, far_down, send, recv):
    e, d = lax.axis_index("expert"), lax.axis_index("dp")
    barrier = pltpu.get_barrier_semaphore()

    def mine(core, low, act):
        pl.when(jnp.logical_and(e % 2 == core, e // 4 % 2 == low))(act)

    for bit, core, low in classes:
        to = flip(e, 1 << bit)

        def hello():
            pl.semaphore_signal(barrier, inc=1, device_id=(to, d), device_id_type=MESH)
            pl.semaphore_wait(barrier, 1)

        def copies():
            return [
                remote(src.at[0], dst, send.at[n], recv.at[n], to, d)
                for n, (src, dst) in enumerate(
                    [(gate, far_gate), (up, far_up), (down, far_down)]
                )
            ]

        def exchange():
            hello()
            for copy in copies():
                copy.start()
            for copy in copies():
                copy.wait()

        mine(core, low, exchange)


def distant_swap(classes, key, near_bits, gate, up, down):
    return pl.pallas_call(
        functools.partial(distant_kernel, classes),
        name="distant",
        out_shape=tuple(jax.ShapeDtypeStruct(w.shape[1:], BF16) for w in (gate, up, down)),
        in_specs=[ANY, ANY, ANY],
        out_specs=(ANY, ANY, ANY),
        scratch_shapes=[pltpu.SemaphoreType.DMA((3,)), pltpu.SemaphoreType.DMA((3,))],
        compiler_params=pltpu.CompilerParams(collective_id=key, has_side_effects=True),
    )(gate, up, down)


def square_body(
    tokens, norm_gain, expert_ids, route_weights, gate_weight, up_weight, down_weight, pair_list
):
    count = lax.axis_size("expert")
    dp = lax.axis_size("dp")
    e, d = lax.axis_index("expert"), lax.axis_index("dp")
    per_device = gate_weight.shape[0]
    rows, top = expert_ids.shape
    width = tokens.shape[1]
    lines = count // 4
    cap = 4 * rows * top // (3 * count * per_device)
    bits = count.bit_length() - 1
    lanes = -(-rows // 128) * 128

    values = tokens.astype(F32)
    scale = lax.rsqrt(jnp.mean(values * values, axis=-1, keepdims=True) + 1e-06)
    normed = (values * scale * norm_gain).astype(BF16)
    meta = jnp.concatenate([expert_ids.astype(BF16), route_weights.astype(BF16)], axis=1)
    meta = jnp.pad(meta.T, ((0, 0), (0, lanes - rows)), constant_values=-1)

    places = jnp.arange(count, dtype=jnp.int32)
    distances = jnp.bitwise_xor(pair_list, places)
    near_bits = min(3, bits)
    kinds = [(0,), (1,), (0, 1)]
    move_sets = [
        [(0, (0, 1))] + [(n + 1, cores) for n, cores in enumerate(picked)]
        for picked in itertools.product(kinds, repeat=near_bits - 1)
    ]
    classes = [
        (bit, core, low)
        for bit in range(near_bits, bits)
        for core in range(2)
        for low in range(2)
    ]
    marks = jnp.zeros_like(places)
    for bit in range(1, near_bits):
        mark = jnp.where(places % 2 == 0, 1, 2) << (2 * (bit - 1))
        marks = jnp.where(distances == (1 << bit), mark, marks)
    for n, (bit, core, low) in enumerate(classes):
        used = (distances == (1 << bit)) & (places % 2 == core) & (places // 4 % 2 == low)
        marks = jnp.where(used, 1 << (2 * (near_bits - 1) + n), marks)
    marks = lax.reduce(marks, jnp.int32(0), lax.bitwise_or, (0,))
    used = [marks >> (2 * n) & 3 for n in range(near_bits - 1)]
    choice = jnp.int32(0)
    for n, mine in enumerate(used):
        others = used[1 - n] if near_bits == 3 else mine
        free = n if n == 0 else 1 - jnp.where(used[0] == 2, 1, 0)
        if n == 0:
            free = jnp.where(others == 1, 1, 0)
        choice = choice * 3 + jnp.where(mine == 0, free, mine - 1)
    far_choice = marks >> (2 * (near_bits - 1))

    def run(moves, key):
        return lambda *args: layer(lines, cap, moves, key, near_bits, *args)

    mixed, got_gate, got_up, got_down = lax.switch(
        choice,
        [run(moves, key) for key, moves in enumerate(move_sets)],
        normed, meta, gate_weight, up_weight, down_weight,
    )
    distance = jnp.bitwise_xor(pair_list[e], e)
    slot = jnp.where(distance >= 4, 2, jnp.where(distance >= 2, 1, 0))

    def held(own, got):
        return jnp.where(distance == 0, own[:1], lax.dynamic_slice_in_dim(got, slot, 1, 0))

    own = (gate_weight, up_weight, down_weight)
    near = (got_gate, got_up, got_down)

    def settled(*args):
        return tuple(held(o, g) for o, g in zip(args[:3], args[3:]))

    def farther(chosen, key):
        def act(*args):
            far = distant_swap(chosen, key, near_bits, *args[:3])
            return tuple(
                jnp.where(distance >= (1 << near_bits), f[None], h)
                for f, h in zip(far, settled(*args))
            )

        return act

    branches = [settled]
    for mask in range(1, 1 << len(classes)):
        chosen = [c for n, c in enumerate(classes) if mask >> n & 1]
        branches.append(farther(chosen, len(move_sets) + mask))
    out = lax.switch(far_choice, branches, *own, *near) if classes else settled(*own, *near)
    return (mixed, *out)


def body(*args):
    dp, count = lax.axis_size("dp"), lax.axis_size("expert")
    per_device = args[4].shape[0]
    rows, top = args[2].shape
    square = dp == 2 and per_device == 2 and count in (8, 16) and rows * top % (3 * count) == 0
    return square_body(*args) if square else wide_body(*args)


def solution(mesh):
    in_specs = (
        P(("expert", "dp"), None),
        P(),
        P(("expert", "dp"), None),
        P(("expert", "dp"), None),
        P("expert", "dp", None),
        P("expert", "dp", None),
        P("expert", "dp", None),
        P(),
    )
    out_specs = (
        P(("expert", "dp"), None),
        P("expert", "dp", None),
        P("expert", "dp", None),
        P("expert", "dp", None),
    )
    return jax.shard_map(body, mesh=mesh, in_specs=in_specs, out_specs=out_specs, check_vma=False)
```

```python
import functools
import itertools

import jax
import jax.numpy as jnp
from jax import lax
from jax.experimental import pallas as pl
from jax.experimental.pallas import tpu as pltpu
from jax.sharding import PartitionSpec as P

F32 = jnp.float32
BF16 = jnp.bfloat16
MESH = pl.DeviceIdType.MESH
ANY = pl.BlockSpec(memory_space=pl.ANY)
INV = pl.BlockSpec(memory_space=pltpu.VMEM)


def bit_route(count, bit, cores):
    return [
        (e, e ^ (1 << bit)) for e in range(count) if e ^ (1 << bit) < count and (e & 1) in cores
    ]


def swap_branch(moves, count):
    def run(blocks, base, distance):
        arrived = [
            [lax.ppermute(b, "expert", bit_route(count, bit, cores)) for b in blocks]
            for bit, cores in moves
        ]
        out = base
        for (bit, _), got in zip(moves, arrived):
            out = [jnp.where(distance == (1 << bit), a, o) for a, o in zip(got, out)]
        return tuple(out)

    return run


def swap(blocks, base, pair_list, count, always, bits):
    mine = lax.axis_index("expert")
    places = jnp.arange(count, dtype=jnp.int32)
    distances = jnp.bitwise_xor(pair_list, places)
    distance = jnp.bitwise_xor(pair_list[mine], mine)
    choice = jnp.int32(0)
    for n, bit in enumerate(bits):
        for core in range(2):
            used = jnp.any((distances == (1 << bit)) & (places & 1 == core)).astype(jnp.int32)
            choice = choice + (used << (2 * n + core))
    branches = []
    for mask in range(1 << (2 * len(bits))):
        moves = [(bit, (0, 1)) for bit in always]
        for n, bit in enumerate(bits):
            cores = tuple(c for c in range(2) if mask >> (2 * n + c) & 1)
            if cores:
                moves.append((bit, cores))
        branches.append(swap_branch(moves, count))
    return list(lax.switch(choice, branches, list(blocks), list(base), distance))


def placing_of(ids, parity, count, per_device, capacity):
    rows = ids.shape[0]
    experts = jnp.arange(count, dtype=jnp.int32) * per_device + parity
    equal = ids[:, :, None] == experts[None, None, :]
    member = jnp.any(equal, axis=1)
    lower = jnp.tril(jnp.ones((rows, rows), BF16), -1)
    rank = jnp.dot(lower, member.astype(BF16), preferred_element_type=F32).astype(jnp.int32)
    rank = jnp.where(member, rank, -1)
    slots = jnp.arange(capacity, dtype=jnp.int32)
    hit = rank.T[:, None, :] == slots[None, :, None]
    return equal, hit


def wide_body(
    tokens, norm_gain, expert_ids, route_weights, gate_weight, up_weight, down_weight, pair_list
):
    count = lax.axis_size("expert")
    dp = lax.axis_size("dp")
    per_device = gate_weight.shape[0]
    group = per_device if dp % per_device == 0 else 1
    experts_all = count * per_device
    rows, top = expert_ids.shape
    width = tokens.shape[1]
    capacity = max(2, 4 * rows * top // (3 * experts_all))
    d = lax.axis_index("dp")
    parity = d % group

    values = tokens.astype(F32)
    scale = lax.rsqrt(jnp.mean(values * values, axis=-1, keepdims=True) + 1e-06)
    normed = (values * scale * norm_gain).astype(BF16)
    route_bf = route_weights.astype(BF16)

    def in_group(block, shift):
        if shift % group == 0:
            return block
        route = [(i, i // group * group + (i % group + shift) % group) for i in range(dp)]
        return lax.ppermute(block, "dp", route)

    token_sets = [
        (in_group(normed, s), in_group(expert_ids, s), in_group(route_bf, s)) for s in range(group)
    ]
    token_sets, weights = lax.optimization_barrier(
        (token_sets, (gate_weight, up_weight, down_weight))
    )

    def shards(weight):
        out = []
        for s in range(dp):
            sent = lax.dynamic_index_in_dim(weight, (d + s) % group, 0, keepdims=False)
            if s:
                sent = lax.ppermute(sent, "dp", [(i, (i + s) % dp) for i in range(dp)])
            out.append(sent)
        return out

    gates, ups, downs = [shards(w) for w in weights]

    outgoing, weightings = [], []
    for normed_s, ids_s, route_s in token_sets:
        equal, hit = placing_of(ids_s, parity, count, per_device, capacity)
        picked = jnp.dot(
            hit.reshape(count * capacity, rows).astype(BF16), normed_s, preferred_element_type=F32
        ).astype(BF16)
        outgoing.append(picked.reshape(count, capacity, width))
        factor = jnp.sum(jnp.where(equal, route_s[:, :, None], jnp.zeros((), BF16)), axis=1)
        weightings.append(
            jnp.where(hit, factor.T[:, None, :], jnp.zeros((), BF16)).reshape(
                count * capacity, rows
            )
        )
    outgoing = jnp.concatenate(outgoing, axis=1)
    bit_total = count.bit_length() - 1
    firsts = [gate_weight[0], up_weight[0], down_weight[0]]
    early = list(range(1, min(3, bit_total)))
    late = list(range(3, bit_total))
    outgoing, pairs = lax.optimization_barrier((outgoing, pair_list))
    received = lax.all_to_all(outgoing, "expert", split_axis=0, concat_axis=0, tiled=True)
    half_held = swap(firsts, firsts, pairs, count, [], early)
    received, half_held = lax.optimization_barrier((received, half_held))
    columns = received.reshape(count * group * capacity, width)

    def times(x, parts):
        size = parts[0].shape[0]
        total = None
        for s, part in enumerate(parts):
            at = (d - s) % dp
            piece = lax.dynamic_slice_in_dim(x, at * size, size, axis=1)
            term = jnp.dot(piece, part, preferred_element_type=F32)
            total = term if total is None else total + term
        return total

    hidden = (jax.nn.silu(times(columns, gates)) * times(columns, ups)).astype(BF16)
    expert_out = times(hidden, downs).astype(BF16)
    expert_out, pairs = lax.optimization_barrier((expert_out, pairs))
    held = swap(firsts, half_held, pairs, count, [0], late)
    returned = lax.all_to_all(
        expert_out.reshape(count, group * capacity, width),
        "expert",
        split_axis=0,
        concat_axis=0,
        tiled=True,
    )
    returned, held = lax.optimization_barrier((returned, held))
    total = None
    for s in range(group):
        part = returned[:, s * capacity : (s + 1) * capacity].reshape(count * capacity, width)
        mix = jnp.einsum("sr,sd->rd", weightings[s], part, preferred_element_type=F32)
        if s:
            mix = in_group(mix.astype(BF16), group - s).astype(F32)
        total = mix if total is None else total + mix
    return (total.astype(BF16), held[0][None], held[1][None], held[2][None])


def flip(index, step):
    return index + step * (1 - 2 * ((index // step) % 2))


def pick(table, index):
    value = jnp.int32(table[0])
    for n in range(1, len(table)):
        value = value + jnp.int32(table[n] - table[0]) * (1 - jnp.minimum(jnp.abs(index - n), 1))
    return value


def near_first(places):
    return [sorted(range(places), key=lambda p: (abs(p - at), p)) for at in range(places)]


def greet(lines, z, e, d):
    barrier = pltpu.get_barrier_semaphore()

    def signal(to_e, to_d):
        pl.semaphore_signal(barrier, inc=1, device_id=(to_e, to_d), device_id_type=MESH)

    signal(e, 1 - d)
    for offset in range(1, 4):
        signal(beside(e, offset), d)
    total = 4 + jnp.minimum(z, 1) + jnp.minimum(lines - 1 - z, 1)

    @pl.when(z > 0)
    def _():
        signal(e - 4, d)

    @pl.when(z < lines - 1)
    def _():
        signal(e + 4, d)

    return total


def beside(e, offset):
    for bit in range(2):
        if offset >> bit & 1:
            e = flip(e, 1 << bit)
    return e


def remote(src, dst, send, recv, to_e, to_d):
    return pltpu.make_async_remote_copy(
        src_ref=src,
        dst_ref=dst,
        send_sem=send,
        recv_sem=recv,
        device_id=(to_e, to_d),
        device_id_type=MESH,
    )


def for_cores(cores, c, act):
    if len(cores) == 2:
        act()
    else:
        pl.when(c == cores[0])(act)


def layer_kernel(
    lines, cap, chunks, lanes, moves, tokens, gain, ids_t, parts_t, gate, up, down,
    mixed, got_gate, got_up, got_down,
    block, meta, stage_in, stage_out, held, metas, chosen, taken, mats, inward, all_down, gates, hidden,
    outs, back, sums, from_left, from_right, total, other,
    k_sem, o_sem, y_send, y_recv, z_send, z_recv, x_send, x_recv,
    b_sem, b_send, b_recv, r_send, r_recv, m_send, m_recv, s_send, s_recv,
):
    e, d = lax.axis_index("expert"), lax.axis_index("dp")
    z, c = e // 4, e % 2
    rows, width = tokens.shape
    top = ids_t.shape[0]
    blocks = 2 * lines
    spare = got_gate.shape[0] - 1
    span = width // chunks
    tile = span
    order = near_first(lines)
    total_greetings = greet(lines, z, e, d)
    values = tokens[...].astype(F32)
    scale = lax.rsqrt(jnp.mean(values * values, axis=-1, keepdims=True) + 1e-06)
    block[...] = (values * scale * gain[...]).astype(BF16)
    meta[...] = jnp.full(meta.shape, -1, BF16)
    tags = jnp.concatenate([ids_t[...].astype(F32), parts_t[...]], axis=0)
    meta[:, :rows] = tags.astype(BF16)
    pl.semaphore_wait(pltpu.get_barrier_semaphore(), total_greetings)

    def across(n):
        pairs = [
            (held.at[z, d], held.at[z, d]),
            (meta, metas.at[z, d]),
            (gate.at[1 - d], inward.at[0, d]),
            (up.at[1 - d], inward.at[1, d]),
        ]
        return remote(*pairs[n], y_send.at[n], y_recv.at[n], e, 1 - d)

    def own(n):
        pairs = [
            (block, held.at[z, d]),
            (meta, metas.at[z, d]),
            (gate.at[d], inward.at[0, d]),
            (up.at[d], inward.at[1, d]),
        ]
        src, dst = pairs[n]
        return pltpu.make_async_copy(src, dst, o_sem.at[n])

    def lower(j, at):
        cols = pl.ds(pl.multiple_of(j * span, span), span)
        return down.at[at, :, cols], all_down.at[j, d]

    def across_lower(j):
        return remote(*lower(j, 1 - d), y_send.at[4 + j], y_recv.at[4 + j], e, 1 - d)

    def own_lower(j):
        return pltpu.make_async_copy(*lower(j, d), o_sem.at[4 + j])

    def keep(n, out):
        src = [gate, up, down][n].at[0]
        dst = [got_gate, got_up, got_down][n].at[spare]
        stage = [stage_in.at[0], stage_in.at[1], stage_out][n]
        pair = (stage, dst) if out else (src, stage)
        return pltpu.make_async_copy(*pair, k_sem.at[n])

    def every(act):
        def one(j, _):
            act(j)
            return 0

        lax.fori_loop(0, chunks, one, 0)

    for n in range(2):
        own(n).start()
    for n in range(2):
        own(n).wait()
    for n in range(4):
        across(n).start()
    every(lambda j: across_lower(j).start())
    for n in range(3):
        keep(n, False).start()

    def further(at, centre):
        return at + (lines - at) * (1 - jnp.minimum(jnp.abs(at - centre), 1))

    def along(way, at, dd):
        to = e + 4 if way else e - 4
        slot = at if way else further(at, z)
        return [
            remote(
                ref.at[at, dd], ref.at[at, dd],
                z_send.at[slot, dd, n], z_recv.at[at, dd, n], to, d,
            )
            for n, ref in enumerate([held, metas])
        ]

    def sideways(at, dd, n):
        return [
            remote(
                chosen.at[n, offset - 1],
                taken.at[offset, at, dd],
                x_send,
                x_recv,
                beside(e, offset),
                d,
            )
            for offset in range(1, 4)
        ]

    def swaps(kind, part):
        src = [gate, up, down][kind]
        dst = [got_gate, got_up, got_down][kind]
        size = src.shape[1] // blocks
        lot = pl.ds(pl.multiple_of(part * size, size), size)
        return [
            (
                remote(
                    src.at[0, lot], dst.at[bit, lot],
                    s_send.at[kind, n], s_recv.at[kind, n],
                    flip(e, 1 << bit), d,
                ),
                bit,
                cores,
            )
            for n, (bit, cores) in enumerate(moves)
        ]

    def swap_start(kind, part, bits):
        for copy, bit, cores in swaps(kind, part):
            if bit in bits:
                for_cores(cores, c, copy.start)

    upper = (
        lax.broadcasted_iota(jnp.int32, (lanes, lanes), 0)
        < lax.broadcasted_iota(jnp.int32, (lanes, lanes), 1)
    ).astype(F32).astype(BF16)
    slots = lax.broadcasted_iota(jnp.int32, (cap, lanes), 0).astype(F32)
    places = lax.broadcasted_iota(jnp.int32, (8, lanes), 0)

    def place(rank):
        at = jnp.int32(0)
        for k in range(lines):
            at = at + (1 - jnp.minimum(jnp.abs(rank - k), 1)) * pick(
                [order[p][k] for p in range(lines)], z
            )
        return at

    def spread(n, _):
        at, dd = place(n // 2), (d + n % 2) % 2

        @pl.when(n == 1)
        def _():
            across(0).wait_recv()
            across(1).wait_recv()

        @pl.when(n > 1)
        def _():
            for copy in along(1, at, dd):
                copy.wait_recv()

        @pl.when(jnp.logical_and(at <= z, z < lines - 1))
        def _():
            for copy in along(1, at, dd):
                copy.start()

        @pl.when(jnp.logical_and(at >= z, z > 0))
        def _():
            for copy in along(0, at, dd):
                copy.start()

        tags = metas[at, dd].astype(F32)
        ids, parts = tags[:top], tags[top:]
        member = jnp.zeros((8, lanes), F32)
        factors = []
        for offset in range(4):
            expert = (2 * beside(e, offset) + d).astype(F32)
            same = ids == expert
            row = jnp.max(jnp.where(same, 1.0, 0.0), axis=0, keepdims=True)
            factors.append(jnp.sum(jnp.where(same, parts, 0.0), axis=0, keepdims=True))
            member = jnp.where(places == offset, row, member)
        rank = jnp.dot(member.astype(BF16), upper, preferred_element_type=F32)
        hits, mixes = [], []
        for offset in range(4):
            hit = jnp.logical_and(
                rank[offset : offset + 1] == slots, member[offset : offset + 1] > 0.5
            )
            hits.append(jnp.where(hit, 1.0, 0.0))
            mixes.append(jnp.where(hit, factors[offset], 0.0))
        hit = jnp.concatenate(hits, axis=0).astype(BF16)[:, :rows]
        mats[at, dd] = jnp.transpose(jnp.concatenate(mixes, axis=0)).astype(BF16)

        def columns(j, _):
            cols = pl.ds(pl.multiple_of(j * tile, tile), tile)
            picked = jnp.dot(
                hit, held[at, dd, :, cols], preferred_element_type=F32
            ).astype(BF16)
            taken[0, at, dd, :, cols] = picked[:cap]
            for offset in range(1, 4):
                chosen[n, offset - 1, :, cols] = picked[offset * cap : (offset + 1) * cap]
            return 0

        lax.fori_loop(0, width // tile, columns, 0)
        for copy in sideways(at, dd, n):
            copy.start()
        swap_start(0, n, (0, 1, 2))
        return 0

    lax.fori_loop(0, blocks, spread, 0)
    for n in range(2, 4):
        own(n).start()
    every(lambda j: own_lower(j).start())
    for n in range(3):
        keep(n, False).wait()
        keep(n, True).start()

    def settle(n, _):
        at, dd = place(n // 2), (d + n % 2) % 2

        @pl.when(jnp.logical_and(at <= z, z < lines - 1))
        def _():
            for copy in along(1, at, dd):
                copy.wait_send()

        @pl.when(jnp.logical_and(at >= z, z > 0))
        def _():
            for copy in along(0, at, dd):
                copy.wait_send()

        swap_start(1, n, (0, 1, 2))
        swap_start(2, n, (0, 2))
        return 0

    lax.fori_loop(0, blocks, settle, 0)
    remote(chosen, chosen, x_send, x_recv, e, 1 - d).wait_send()
    rest = taken.at[pl.ds(1, 3)]
    remote(rest, rest, x_send, x_recv, e, 1 - d).wait_recv()
    lot = blocks * cap

    inner = hidden.shape[-1]
    wide = inner // 2 if inner % 256 == 0 else inner
    tiles = inner // wide

    def project(kind, _):
        for n in range(2):

            @pl.when(kind == n)
            def _():
                own(2 + n).wait()
                across(2 + n).wait()

        def one(i, _):
            offset = i // tiles
            cols = pl.ds(pl.multiple_of(i % tiles * wide, wide), wide)
            value = jnp.dot(
                taken[offset].reshape(lot, width),
                inward[kind, :, :, cols].reshape(width, wide),
                preferred_element_type=F32,
            )

            @pl.when(kind == 0)
            def _():
                gates[offset, :, cols] = value / (1.0 + jnp.exp(-value))

            @pl.when(kind == 1)
            def _():
                hidden[offset, :, cols] = (gates[offset, :, cols] * value).astype(BF16)

            return 0

        return lax.fori_loop(0, 4 * tiles, one, 0)

    lax.fori_loop(0, 2, project, 0)
    every(lambda j: own_lower(j).wait())

    def distant(k):
        return place(lines - 1 - k)

    def local(j):
        return pltpu.make_async_copy(outs.at[j, 0], back.at[j, :, :, 0], b_sem.at[j])

    def homeward(j, at):
        return [
            remote(
                outs.at[j, offset, at],
                back.at[j, at, :, offset],
                b_send.at[j],
                b_recv.at[j, at],
                beside(e, offset),
                d,
            )
            for offset in range(1, 4)
        ]

    def reduced(way, j, at, here):
        to = e + 4 if way else e - 4
        land = from_left if way else from_right
        slot = at if way else further(at, here)
        return remote(
            sums.at[j, at], land.at[j, at], r_send.at[j], r_recv.at[j, slot], to, d
        )

    def exchanged(j):
        return remote(
            sums.at[j, z, 1 - d], other.at[j], m_send.at[j], m_recv.at[j], e, 1 - d
        )

    def produce(j):
        across_lower(j).wait()

        def one(i, _):
            offset = i // (span // tile)
            cols = pl.ds(pl.multiple_of(i % (span // tile) * tile, tile), tile)
            out = jnp.dot(
                hidden[offset],
                all_down[j, :, :, cols].reshape(inner, tile),
                preferred_element_type=F32,
            )
            outs[j, offset, :, :, :, cols] = out.astype(BF16).reshape(lines, 2, cap, tile)
            return 0

        lax.fori_loop(0, 4 * (span // tile), one, 0)
        local(j).start()

        def send(k, _):
            at = distant(k)
            for copy in homeward(j, at):
                copy.start()
            return 0

        lax.fori_loop(0, lines, send, 0)

    def reduce(i):
        def one(n, _):
            k = lines - 1 - n
            j = i - 1 - k

            @pl.when(jnp.logical_and(j >= 0, j < chunks))
            def _():
                step(j, k)

            return 0

        def step(j, k):
            @pl.when(k == 0)
            def _():
                local(j).wait()

            at = distant(k)
            come = back.at[j, at, :, pl.ds(1, 3)]
            remote(come, come, b_send.at[j], b_recv.at[j, at], e, 1 - d).wait_recv()
            left = jnp.logical_and(at >= z, z > 0)
            right = jnp.logical_and(at <= z, z < lines - 1)

            @pl.when(left)
            def _():
                reduced(1, j, at, z).wait_recv()

            @pl.when(right)
            def _():
                reduced(0, j, at, z).wait_recv()

            def piece(i, _):
                dd = i // (span // tile)
                cols = pl.ds(pl.multiple_of(i % (span // tile) * tile, tile), tile)
                total[...] = jnp.dot(
                    mats[at, dd, :rows],
                    back[j, at, dd, :, :, cols].reshape(4 * cap, tile),
                    preferred_element_type=F32,
                )

                @pl.when(left)
                def _():
                    total[...] += from_left[j, at, dd, :, cols].astype(F32)

                @pl.when(right)
                def _():
                    total[...] += from_right[j, at, dd, :, cols].astype(F32)

                sums[j, at, dd, :, cols] = total[...].astype(BF16)
                return 0

            lax.fori_loop(0, 2 * (span // tile), piece, 0)

            @pl.when(at > z)
            def _():
                reduced(1, j, at, z).start()

            @pl.when(at < z)
            def _():
                reduced(0, j, at, z - 1).start()

            @pl.when(k == lines - 1)
            def _():
                exchanged(j).start()

        lax.fori_loop(0, lines, one, 0)

    def turn(i, _):
        @pl.when(i < chunks)
        def _():
            produce(i)

        @pl.when(i == chunks - 1)
        def _():
            lax.fori_loop(0, blocks, lambda n, _: swap_start(2, n, (1,)) or 0, 0)

        reduce(i)
        return 0

    lax.fori_loop(0, chunks + lines, turn, 0)

    def close(j, _):
        exchanged(j).wait()
        cols = pl.ds(pl.multiple_of(j * span, span), span)
        mixed[:, cols] = (sums[j, z, d].astype(F32) + other[j].astype(F32)).astype(BF16)

        gone = sums.at[j, pl.ds(0, lines - 1)]
        remote(gone, gone, r_send.at[j], m_recv.at[j], e, 1 - d).wait_send()
        gone = outs.at[j, pl.ds(1, 3)]
        remote(gone, gone, b_send.at[j], m_recv.at[j], e, 1 - d).wait_send()
        return 0

    lax.fori_loop(0, chunks, close, 0)
    across(0).wait_send()
    across(1).wait_send()
    for n in range(3):
        keep(n, True).wait()

    for kind, (src, dst) in enumerate([(gate, got_gate), (up, got_up), (down, got_down)]):
        for n, (bit, cores) in enumerate(moves):
            copy = remote(
                src.at[0], dst.at[bit], s_send.at[kind, n], s_recv.at[kind, n], e, 1 - d
            )
            for_cores(cores, c, copy.wait)


def layer(lines, cap, moves, key, bits, tokens, gain, ids_t, parts_t, gate, up, down):
    rows, width = tokens.shape
    top = ids_t.shape[0]
    lanes = -(-rows // 128) * 128
    blocks = 2 * lines
    half, inner = gate.shape[1:]
    chunks = 4
    span = width // chunks
    tile = span
    part = (chunks, lines, 2, rows, span)
    sem = pltpu.SemaphoreType.DMA
    return pl.pallas_call(
        functools.partial(layer_kernel, lines, cap, chunks, lanes, moves),
        name="layer",
        out_shape=(
            jax.ShapeDtypeStruct((rows, width), BF16),
            jax.ShapeDtypeStruct((bits + 1, half, inner), BF16),
            jax.ShapeDtypeStruct((bits + 1, half, inner), BF16),
            jax.ShapeDtypeStruct((bits + 1,) + down.shape[1:], BF16),
        ),
        in_specs=[INV, INV, INV, INV, ANY, ANY, ANY],
        out_specs=(INV, ANY, ANY, ANY),
        scratch_shapes=[
            pltpu.VMEM((rows, width), BF16),
            pltpu.VMEM((2 * top, lanes), BF16),
            pltpu.VMEM((2, half, inner), BF16),
            pltpu.VMEM(down.shape[1:], BF16),
            pltpu.VMEM((lines, 2, rows, width), BF16),
            pltpu.VMEM((lines, 2, 2 * top, lanes), BF16),
            pltpu.VMEM((blocks, 3, cap, width), BF16),
            pltpu.VMEM((4, lines, 2, cap, width), BF16),
            pltpu.VMEM((lines, 2, lanes, 4 * cap), BF16),
            pltpu.VMEM((2, 2, half, inner), BF16),
            pltpu.VMEM((chunks, 2, down.shape[1], span), BF16),
            pltpu.VMEM((4, blocks * cap, inner), F32),
            pltpu.VMEM((4, blocks * cap, inner), BF16),
            pltpu.VMEM((chunks, 4, lines, 2, cap, span), BF16),
            pltpu.VMEM((chunks, lines, 2, 4, cap, span), BF16),
            pltpu.VMEM(part, BF16),
            pltpu.VMEM(part, BF16),
            pltpu.VMEM(part, BF16),
            pltpu.VMEM((rows, tile), F32),
            pltpu.VMEM((chunks, rows, span), BF16),
            sem((3,)),
            sem((4 + chunks,)),
            sem((4 + chunks,)),
            sem((4 + chunks,)),
            sem((lines + 1, 2, 2)),
            sem((lines, 2, 2)),
            sem,
            sem,
            sem((chunks,)),
            sem((chunks,)),
            sem((chunks, lines)),
            sem((chunks,)),
            sem((chunks, lines + 1)),
            sem((chunks,)),
            sem((chunks,)),
            sem((3, len(moves))),
            sem((3, len(moves))),
        ],
        compiler_params=pltpu.CompilerParams(
            collective_id=key, has_side_effects=True, vmem_limit_bytes=60 << 20
        ),
    )(tokens, gain, ids_t, parts_t, gate, up, down)


def distant_kernel(classes, gate, up, down, far_gate, far_up, far_down, send, recv):
    e, d = lax.axis_index("expert"), lax.axis_index("dp")
    barrier = pltpu.get_barrier_semaphore()

    def mine(core, low, act):
        pl.when(jnp.logical_and(e % 2 == core, e // 4 % 2 == low))(act)

    for bit, core, low in classes:
        to = flip(e, 1 << bit)

        def hello():
            pl.semaphore_signal(barrier, inc=1, device_id=(to, d), device_id_type=MESH)
            pl.semaphore_wait(barrier, 1)

        def copies():
            return [
                remote(src.at[0], dst, send.at[n], recv.at[n], to, d)
                for n, (src, dst) in enumerate(
                    [(gate, far_gate), (up, far_up), (down, far_down)]
                )
            ]

        def exchange():
            hello()
            for copy in copies():
                copy.start()
            for copy in copies():
                copy.wait()

        mine(core, low, exchange)


def distant_swap(classes, key, near_bits, gate, up, down):
    return pl.pallas_call(
        functools.partial(distant_kernel, classes),
        name="distant",
        out_shape=tuple(jax.ShapeDtypeStruct(w.shape[1:], BF16) for w in (gate, up, down)),
        in_specs=[ANY, ANY, ANY],
        out_specs=(ANY, ANY, ANY),
        scratch_shapes=[pltpu.SemaphoreType.DMA((3,)), pltpu.SemaphoreType.DMA((3,))],
        compiler_params=pltpu.CompilerParams(collective_id=key, has_side_effects=True),
    )(gate, up, down)


def square_body(
    tokens, norm_gain, expert_ids, route_weights, gate_weight, up_weight, down_weight, pair_list
):
    count = lax.axis_size("expert")
    dp = lax.axis_size("dp")
    e, d = lax.axis_index("expert"), lax.axis_index("dp")
    per_device = gate_weight.shape[0]
    rows, top = expert_ids.shape
    width = tokens.shape[1]
    lines = count // 4
    cap = 4 * rows * top // (3 * count * per_device)
    bits = count.bit_length() - 1
    places = jnp.arange(count, dtype=jnp.int32)
    distances = jnp.bitwise_xor(pair_list, places)
    near_bits = min(3, bits)
    kinds = [(0,), (1,), (0, 1)]
    move_sets = [
        [(0, (0, 1))] + [(n + 1, cores) for n, cores in enumerate(picked)]
        for picked in itertools.product(kinds, repeat=near_bits - 1)
    ]
    classes = [
        (bit, core, low)
        for bit in range(near_bits, bits)
        for core in range(2)
        for low in range(2)
    ]
    marks = jnp.zeros_like(places)
    for bit in range(1, near_bits):
        mark = jnp.where(places % 2 == 0, 1, 2) << (2 * (bit - 1))
        marks = jnp.where(distances == (1 << bit), mark, marks)
    for n, (bit, core, low) in enumerate(classes):
        used = (distances == (1 << bit)) & (places % 2 == core) & (places // 4 % 2 == low)
        marks = jnp.where(used, 1 << (2 * (near_bits - 1) + n), marks)
    marks = lax.reduce(marks, jnp.int32(0), lax.bitwise_or, (0,))
    used = [marks >> (2 * n) & 3 for n in range(near_bits - 1)]
    choice = jnp.int32(0)
    for n, mine in enumerate(used):
        others = used[1 - n] if near_bits == 3 else mine
        free = n if n == 0 else 1 - jnp.where(used[0] == 2, 1, 0)
        if n == 0:
            free = jnp.where(others == 1, 1, 0)
        choice = choice * 3 + jnp.where(mine == 0, free, mine - 1)
    far_choice = marks >> (2 * (near_bits - 1))

    def run(moves, key):
        return lambda *args: layer(lines, cap, moves, key, near_bits, *args)

    mixed, got_gate, got_up, got_down = lax.switch(
        choice,
        [run(moves, key) for key, moves in enumerate(move_sets)],
        tokens, norm_gain[None], expert_ids.T, route_weights.T, gate_weight, up_weight, down_weight,
    )
    distance = jnp.bitwise_xor(pair_list[e], e)
    slot = jnp.where(distance >= 4, 2, jnp.where(distance >= 2, 1, 0))
    slot = jnp.where(distance == 0, near_bits, slot)

    def held(got):
        return lax.dynamic_slice_in_dim(got, slot, 1, 0)

    own = (gate_weight, up_weight, down_weight)
    near = (got_gate, got_up, got_down)

    def settled(*args):
        return tuple(held(got) for got in args[3:])

    def farther(chosen, key):
        def act(*args):
            far = distant_swap(chosen, key, near_bits, *args[:3])
            return tuple(
                jnp.where(distance >= (1 << near_bits), f[None], h)
                for f, h in zip(far, settled(*args))
            )

        return act

    branches = [settled]
    for mask in range(1, 1 << len(classes)):
        chosen = [c for n, c in enumerate(classes) if mask >> n & 1]
        branches.append(farther(chosen, len(move_sets) + mask))
    out = lax.switch(far_choice, branches, *own, *near) if classes else settled(*own, *near)
    return (mixed, *out)


def body(*args):
    dp, count = lax.axis_size("dp"), lax.axis_size("expert")
    per_device = args[4].shape[0]
    rows, top = args[2].shape
    square = dp == 2 and per_device == 2 and count in (8, 16) and rows * top % (3 * count) == 0
    return square_body(*args) if square else wide_body(*args)


def solution(mesh):
    in_specs = (
        P(("expert", "dp"), None),
        P(),
        P(("expert", "dp"), None),
        P(("expert", "dp"), None),
        P("expert", "dp", None),
        P("expert", "dp", None),
        P("expert", "dp", None),
        P(),
    )
    out_specs = (
        P(("expert", "dp"), None),
        P("expert", "dp", None),
        P("expert", "dp", None),
        P("expert", "dp", None),
    )
    return jax.shard_map(body, mesh=mesh, in_specs=in_specs, out_specs=out_specs, check_vma=False)
```

```python
import functools
import itertools

import jax
import jax.numpy as jnp
from jax import lax
from jax.experimental import pallas as pl
from jax.experimental.pallas import tpu as pltpu
from jax.sharding import PartitionSpec as P

F32 = jnp.float32
BF16 = jnp.bfloat16
MESH = pl.DeviceIdType.MESH
ANY = pl.BlockSpec(memory_space=pl.ANY)
INV = pl.BlockSpec(memory_space=pltpu.VMEM)


def bit_route(count, bit, cores):
    return [
        (e, e ^ (1 << bit)) for e in range(count) if e ^ (1 << bit) < count and (e & 1) in cores
    ]


def swap_branch(moves, count):
    def run(blocks, base, distance):
        arrived = [
            [lax.ppermute(b, "expert", bit_route(count, bit, cores)) for b in blocks]
            for bit, cores in moves
        ]
        out = base
        for (bit, _), got in zip(moves, arrived):
            out = [jnp.where(distance == (1 << bit), a, o) for a, o in zip(got, out)]
        return tuple(out)

    return run


def swap(blocks, base, pair_list, count, always, bits):
    mine = lax.axis_index("expert")
    places = jnp.arange(count, dtype=jnp.int32)
    distances = jnp.bitwise_xor(pair_list, places)
    distance = jnp.bitwise_xor(pair_list[mine], mine)
    choice = jnp.int32(0)
    for n, bit in enumerate(bits):
        for core in range(2):
            used = jnp.any((distances == (1 << bit)) & (places & 1 == core)).astype(jnp.int32)
            choice = choice + (used << (2 * n + core))
    branches = []
    for mask in range(1 << (2 * len(bits))):
        moves = [(bit, (0, 1)) for bit in always]
        for n, bit in enumerate(bits):
            cores = tuple(c for c in range(2) if mask >> (2 * n + c) & 1)
            if cores:
                moves.append((bit, cores))
        branches.append(swap_branch(moves, count))
    return list(lax.switch(choice, branches, list(blocks), list(base), distance))


def placing_of(ids, parity, count, per_device, capacity):
    rows = ids.shape[0]
    experts = jnp.arange(count, dtype=jnp.int32) * per_device + parity
    equal = ids[:, :, None] == experts[None, None, :]
    member = jnp.any(equal, axis=1)
    lower = jnp.tril(jnp.ones((rows, rows), BF16), -1)
    rank = jnp.dot(lower, member.astype(BF16), preferred_element_type=F32).astype(jnp.int32)
    rank = jnp.where(member, rank, -1)
    slots = jnp.arange(capacity, dtype=jnp.int32)
    hit = rank.T[:, None, :] == slots[None, :, None]
    return equal, hit


def wide_body(
    tokens, norm_gain, expert_ids, route_weights, gate_weight, up_weight, down_weight, pair_list
):
    count = lax.axis_size("expert")
    dp = lax.axis_size("dp")
    per_device = gate_weight.shape[0]
    group = per_device if dp % per_device == 0 else 1
    experts_all = count * per_device
    rows, top = expert_ids.shape
    width = tokens.shape[1]
    capacity = max(2, 4 * rows * top // (3 * experts_all))
    d = lax.axis_index("dp")
    parity = d % group

    values = tokens.astype(F32)
    scale = lax.rsqrt(jnp.mean(values * values, axis=-1, keepdims=True) + 1e-06)
    normed = (values * scale * norm_gain).astype(BF16)
    route_bf = route_weights.astype(BF16)

    def in_group(block, shift):
        if shift % group == 0:
            return block
        route = [(i, i // group * group + (i % group + shift) % group) for i in range(dp)]
        return lax.ppermute(block, "dp", route)

    token_sets = [
        (in_group(normed, s), in_group(expert_ids, s), in_group(route_bf, s)) for s in range(group)
    ]
    token_sets, weights = lax.optimization_barrier(
        (token_sets, (gate_weight, up_weight, down_weight))
    )

    def shards(weight):
        out = []
        for s in range(dp):
            sent = lax.dynamic_index_in_dim(weight, (d + s) % group, 0, keepdims=False)
            if s:
                sent = lax.ppermute(sent, "dp", [(i, (i + s) % dp) for i in range(dp)])
            out.append(sent)
        return out

    gates, ups, downs = [shards(w) for w in weights]

    outgoing, weightings = [], []
    for normed_s, ids_s, route_s in token_sets:
        equal, hit = placing_of(ids_s, parity, count, per_device, capacity)
        picked = jnp.dot(
            hit.reshape(count * capacity, rows).astype(BF16), normed_s, preferred_element_type=F32
        ).astype(BF16)
        outgoing.append(picked.reshape(count, capacity, width))
        factor = jnp.sum(jnp.where(equal, route_s[:, :, None], jnp.zeros((), BF16)), axis=1)
        weightings.append(
            jnp.where(hit, factor.T[:, None, :], jnp.zeros((), BF16)).reshape(
                count * capacity, rows
            )
        )
    outgoing = jnp.concatenate(outgoing, axis=1)
    bit_total = count.bit_length() - 1
    firsts = [gate_weight[0], up_weight[0], down_weight[0]]
    early = list(range(1, min(3, bit_total)))
    late = list(range(3, bit_total))
    outgoing, pairs = lax.optimization_barrier((outgoing, pair_list))
    received = lax.all_to_all(outgoing, "expert", split_axis=0, concat_axis=0, tiled=True)
    half_held = swap(firsts, firsts, pairs, count, [], early)
    received, half_held = lax.optimization_barrier((received, half_held))
    columns = received.reshape(count * group * capacity, width)

    def times(x, parts):
        size = parts[0].shape[0]
        total = None
        for s, part in enumerate(parts):
            at = (d - s) % dp
            piece = lax.dynamic_slice_in_dim(x, at * size, size, axis=1)
            term = jnp.dot(piece, part, preferred_element_type=F32)
            total = term if total is None else total + term
        return total

    hidden = (jax.nn.silu(times(columns, gates)) * times(columns, ups)).astype(BF16)
    expert_out = times(hidden, downs).astype(BF16)
    expert_out, pairs = lax.optimization_barrier((expert_out, pairs))
    held = swap(firsts, half_held, pairs, count, [0], late)
    returned = lax.all_to_all(
        expert_out.reshape(count, group * capacity, width),
        "expert",
        split_axis=0,
        concat_axis=0,
        tiled=True,
    )
    returned, held = lax.optimization_barrier((returned, held))
    total = None
    for s in range(group):
        part = returned[:, s * capacity : (s + 1) * capacity].reshape(count * capacity, width)
        mix = jnp.einsum("sr,sd->rd", weightings[s], part, preferred_element_type=F32)
        if s:
            mix = in_group(mix.astype(BF16), group - s).astype(F32)
        total = mix if total is None else total + mix
    return (total.astype(BF16), held[0][None], held[1][None], held[2][None])


def flip(index, step):
    return index + step * (1 - 2 * ((index // step) % 2))


def pick(table, index):
    value = jnp.int32(table[0])
    for n in range(1, len(table)):
        value = value + jnp.int32(table[n] - table[0]) * (1 - jnp.minimum(jnp.abs(index - n), 1))
    return value


def near_first(places):
    return [sorted(range(places), key=lambda p: (abs(p - at), p)) for at in range(places)]


def greet(lines, z, e, d):
    barrier = pltpu.get_barrier_semaphore()

    def signal(to_e, to_d):
        pl.semaphore_signal(barrier, inc=1, device_id=(to_e, to_d), device_id_type=MESH)

    signal(e, 1 - d)
    for offset in range(1, 4):
        signal(beside(e, offset), d)
    total = 4 + jnp.minimum(z, 1) + jnp.minimum(lines - 1 - z, 1)

    @pl.when(z > 0)
    def _():
        signal(e - 4, d)

    @pl.when(z < lines - 1)
    def _():
        signal(e + 4, d)

    return total


def beside(e, offset):
    for bit in range(2):
        if offset >> bit & 1:
            e = flip(e, 1 << bit)
    return e


def remote(src, dst, send, recv, to_e, to_d):
    return pltpu.make_async_remote_copy(
        src_ref=src,
        dst_ref=dst,
        send_sem=send,
        recv_sem=recv,
        device_id=(to_e, to_d),
        device_id_type=MESH,
    )


def for_cores(cores, c, act):
    if len(cores) == 2:
        act()
    else:
        pl.when(c == cores[0])(act)


def layer_kernel(
    lines, cap, chunks, lanes, moves, tokens, gain, ids_t, parts_t, gate, up, down,
    mixed, got_gate, got_up, got_down,
    block, meta, stage_in, stage_out, held, metas, chosen, taken, mats, inward, all_down, gates, hidden,
    outs, back, sums, from_left, from_right, total, other,
    k_sem, o_sem, y_send, y_recv, z_send, z_recv, x_send, x_recv,
    b_sem, b_send, b_recv, r_send, r_recv, m_send, m_recv, s_send, s_recv,
):
    e, d = lax.axis_index("expert"), lax.axis_index("dp")
    z, c = e // 4, e % 2
    rows, width = tokens.shape
    top = ids_t.shape[0]
    blocks = 2 * lines
    spare = got_gate.shape[0] - 1
    span = width // chunks
    tile = span
    order = near_first(lines)
    total_greetings = greet(lines, z, e, d)
    values = tokens[...].astype(F32)
    scale = lax.rsqrt(jnp.mean(values * values, axis=-1, keepdims=True) + 1e-06)
    block[...] = (values * scale * gain[...]).astype(BF16)
    meta[...] = jnp.full(meta.shape, -1, BF16)
    tags = jnp.concatenate([ids_t[...].astype(F32), parts_t[...]], axis=0)
    meta[:, :rows] = tags.astype(BF16)
    pl.semaphore_wait(pltpu.get_barrier_semaphore(), total_greetings)

    def across(n):
        pairs = [
            (held.at[z, d], held.at[z, d]),
            (meta, metas.at[z, d]),
            (gate.at[1 - d], inward.at[0, d]),
            (up.at[1 - d], inward.at[1, d]),
        ]
        return remote(*pairs[n], y_send.at[n], y_recv.at[n], e, 1 - d)

    def own(n):
        pairs = [
            (block, held.at[z, d]),
            (meta, metas.at[z, d]),
            (gate.at[d], inward.at[0, d]),
            (up.at[d], inward.at[1, d]),
        ]
        src, dst = pairs[n]
        return pltpu.make_async_copy(src, dst, o_sem.at[n])

    def lower(j, at):
        cols = pl.ds(pl.multiple_of(j * span, span), span)
        return down.at[at, :, cols], all_down.at[j, d]

    def across_lower(j):
        return remote(*lower(j, 1 - d), y_send.at[4 + j], y_recv.at[4 + j], e, 1 - d)

    def own_lower(j):
        return pltpu.make_async_copy(*lower(j, d), o_sem.at[4 + j])

    def keep(n, out):
        src = [gate, up, down][n].at[0]
        dst = [got_gate, got_up, got_down][n].at[spare]
        stage = [stage_in.at[0], stage_in.at[1], stage_out][n]
        pair = (stage, dst) if out else (src, stage)
        return pltpu.make_async_copy(*pair, k_sem.at[n])

    def every(act):
        def one(j, _):
            act(j)
            return 0

        lax.fori_loop(0, chunks, one, 0)

    for n in range(2):
        own(n).start()
    for n in range(2):
        own(n).wait()
    for n in range(4):
        across(n).start()
    every(lambda j: across_lower(j).start())
    for n in range(3):
        keep(n, False).start()

    def further(at, centre):
        return at + (lines - at) * (1 - jnp.minimum(jnp.abs(at - centre), 1))

    def along(way, at, dd):
        to = e + 4 if way else e - 4
        slot = at if way else further(at, z)
        return [
            remote(
                ref.at[at, dd], ref.at[at, dd],
                z_send.at[slot, dd, n], z_recv.at[at, dd, n], to, d,
            )
            for n, ref in enumerate([held, metas])
        ]

    def sideways(at, dd, n):
        return [
            remote(
                chosen.at[n, offset - 1],
                taken.at[offset, at, dd],
                x_send,
                x_recv,
                beside(e, offset),
                d,
            )
            for offset in range(1, 4)
        ]

    def swaps(kind, part):
        src = [gate, up, down][kind]
        dst = [got_gate, got_up, got_down][kind]
        size = src.shape[1] // blocks
        lot = pl.ds(pl.multiple_of(part * size, size), size)
        return [
            (
                remote(
                    src.at[0, lot], dst.at[bit, lot],
                    s_send.at[kind, n], s_recv.at[kind, n],
                    flip(e, 1 << bit), d,
                ),
                bit,
                cores,
            )
            for n, (bit, cores) in enumerate(moves)
        ]

    def swap_start(kind, part, bits):
        for copy, bit, cores in swaps(kind, part):
            if bit in bits:
                for_cores(cores, c, copy.start)

    upper = (
        lax.broadcasted_iota(jnp.int32, (lanes, lanes), 0)
        < lax.broadcasted_iota(jnp.int32, (lanes, lanes), 1)
    ).astype(F32).astype(BF16)
    slots = lax.broadcasted_iota(jnp.int32, (cap, lanes), 0).astype(F32)
    places = lax.broadcasted_iota(jnp.int32, (8, lanes), 0)

    def place(rank):
        at = jnp.int32(0)
        for k in range(lines):
            at = at + (1 - jnp.minimum(jnp.abs(rank - k), 1)) * pick(
                [order[p][k] for p in range(lines)], z
            )
        return at

    def spread(n, _):
        at, dd = place(n // 2), (d + n % 2) % 2

        @pl.when(n == 1)
        def _():
            across(0).wait_recv()
            across(1).wait_recv()

        @pl.when(n > 1)
        def _():
            for copy in along(1, at, dd):
                copy.wait_recv()

        @pl.when(jnp.logical_and(at <= z, z < lines - 1))
        def _():
            for copy in along(1, at, dd):
                copy.start()

        @pl.when(jnp.logical_and(at >= z, z > 0))
        def _():
            for copy in along(0, at, dd):
                copy.start()

        tags = metas[at, dd].astype(F32)
        ids, parts = tags[:top], tags[top:]
        member = jnp.zeros((8, lanes), F32)
        factors = []
        for offset in range(4):
            expert = (2 * beside(e, offset) + d).astype(F32)
            same = ids == expert
            row = jnp.max(jnp.where(same, 1.0, 0.0), axis=0, keepdims=True)
            factors.append(jnp.sum(jnp.where(same, parts, 0.0), axis=0, keepdims=True))
            member = jnp.where(places == offset, row, member)
        rank = jnp.dot(member.astype(BF16), upper, preferred_element_type=F32)
        hits, mixes = [], []
        for offset in range(4):
            hit = jnp.logical_and(
                rank[offset : offset + 1] == slots, member[offset : offset + 1] > 0.5
            )
            hits.append(jnp.where(hit, 1.0, 0.0))
            mixes.append(jnp.where(hit, factors[offset], 0.0))
        hit = jnp.concatenate(hits, axis=0).astype(BF16)[:, :rows]
        mats[at, dd] = jnp.transpose(jnp.concatenate(mixes, axis=0)).astype(BF16)

        def columns(j, _):
            cols = pl.ds(pl.multiple_of(j * tile, tile), tile)
            picked = jnp.dot(
                hit, held[at, dd, :, cols], preferred_element_type=F32
            ).astype(BF16)
            taken[0, at, dd, :, cols] = picked[:cap]
            for offset in range(1, 4):
                chosen[n, offset - 1, :, cols] = picked[offset * cap : (offset + 1) * cap]
            return 0

        lax.fori_loop(0, width // tile, columns, 0)
        for copy in sideways(at, dd, n):
            copy.start()
        swap_start(0, n, (0, 1, 2))
        return 0

    lax.fori_loop(0, blocks, spread, 0)
    for n in range(2, 4):
        own(n).start()
    every(lambda j: own_lower(j).start())
    for n in range(3):
        keep(n, False).wait()
        keep(n, True).start()

    def settle(n, _):
        at, dd = place(n // 2), (d + n % 2) % 2

        @pl.when(jnp.logical_and(at <= z, z < lines - 1))
        def _():
            for copy in along(1, at, dd):
                copy.wait_send()

        @pl.when(jnp.logical_and(at >= z, z > 0))
        def _():
            for copy in along(0, at, dd):
                copy.wait_send()

        swap_start(1, n, (0, 1, 2))
        swap_start(2, n, (0, 2))
        return 0

    lax.fori_loop(0, blocks, settle, 0)
    remote(chosen, chosen, x_send, x_recv, e, 1 - d).wait_send()
    rest = taken.at[pl.ds(1, 3)]
    remote(rest, rest, x_send, x_recv, e, 1 - d).wait_recv()
    lot = blocks * cap

    inner = hidden.shape[-1]
    wide = inner // 3 if inner % 384 == 0 else inner
    tiles = inner // wide

    def project(kind, _):
        for n in range(2):

            @pl.when(kind == n)
            def _():
                own(2 + n).wait()
                across(2 + n).wait()

        def one(i, _):
            offset = i // tiles
            cols = pl.ds(pl.multiple_of(i % tiles * wide, wide), wide)
            value = jnp.dot(
                taken[offset].reshape(lot, width),
                inward[kind, :, :, cols].reshape(width, wide),
                preferred_element_type=F32,
            )

            @pl.when(kind == 0)
            def _():
                gates[offset, :, cols] = value / (1.0 + jnp.exp(-value))

            @pl.when(kind == 1)
            def _():
                hidden[offset, :, cols] = (gates[offset, :, cols] * value).astype(BF16)

            return 0

        return lax.fori_loop(0, 4 * tiles, one, 0)

    lax.fori_loop(0, 2, project, 0)
    every(lambda j: own_lower(j).wait())

    def distant(k):
        return place(lines - 1 - k)

    def local(j):
        return pltpu.make_async_copy(outs.at[j, 0], back.at[j, :, :, 0], b_sem.at[j])

    def homeward(j, at):
        return [
            remote(
                outs.at[j, offset, at],
                back.at[j, at, :, offset],
                b_send.at[j],
                b_recv.at[j, at],
                beside(e, offset),
                d,
            )
            for offset in range(1, 4)
        ]

    def reduced(way, j, at, here):
        to = e + 4 if way else e - 4
        land = from_left if way else from_right
        slot = at if way else further(at, here)
        return remote(
            sums.at[j, at], land.at[j, at], r_send.at[j], r_recv.at[j, slot], to, d
        )

    def exchanged(j):
        return remote(
            sums.at[j, z, 1 - d], other.at[j], m_send.at[j], m_recv.at[j], e, 1 - d
        )

    def produce(j):
        across_lower(j).wait()

        def one(i, _):
            offset = i // (span // tile)
            cols = pl.ds(pl.multiple_of(i % (span // tile) * tile, tile), tile)
            out = jnp.dot(
                hidden[offset],
                all_down[j, :, :, cols].reshape(inner, tile),
                preferred_element_type=F32,
            )
            outs[j, offset, :, :, :, cols] = out.astype(BF16).reshape(lines, 2, cap, tile)
            return 0

        lax.fori_loop(0, 4 * (span // tile), one, 0)
        local(j).start()

        def send(k, _):
            at = distant(k)
            for copy in homeward(j, at):
                copy.start()
            return 0

        lax.fori_loop(0, lines, send, 0)

    def reduce(i):
        def one(n, _):
            k = lines - 1 - n
            j = i - 1 - k

            @pl.when(jnp.logical_and(j >= 0, j < chunks))
            def _():
                step(j, k)

            return 0

        def step(j, k):
            @pl.when(k == 0)
            def _():
                local(j).wait()

            at = distant(k)
            come = back.at[j, at, :, pl.ds(1, 3)]
            remote(come, come, b_send.at[j], b_recv.at[j, at], e, 1 - d).wait_recv()
            left = jnp.logical_and(at >= z, z > 0)
            right = jnp.logical_and(at <= z, z < lines - 1)

            @pl.when(left)
            def _():
                reduced(1, j, at, z).wait_recv()

            @pl.when(right)
            def _():
                reduced(0, j, at, z).wait_recv()

            def piece(i, _):
                dd = i // (span // tile)
                cols = pl.ds(pl.multiple_of(i % (span // tile) * tile, tile), tile)
                total[...] = jnp.dot(
                    mats[at, dd, :rows],
                    back[j, at, dd, :, :, cols].reshape(4 * cap, tile),
                    preferred_element_type=F32,
                )

                @pl.when(left)
                def _():
                    total[...] += from_left[j, at, dd, :, cols].astype(F32)

                @pl.when(right)
                def _():
                    total[...] += from_right[j, at, dd, :, cols].astype(F32)

                sums[j, at, dd, :, cols] = total[...].astype(BF16)
                return 0

            lax.fori_loop(0, 2 * (span // tile), piece, 0)

            @pl.when(at > z)
            def _():
                reduced(1, j, at, z).start()

            @pl.when(at < z)
            def _():
                reduced(0, j, at, z - 1).start()

            @pl.when(k == lines - 1)
            def _():
                exchanged(j).start()

        lax.fori_loop(0, lines, one, 0)

    def turn(i, _):
        @pl.when(i < chunks)
        def _():
            produce(i)

        @pl.when(i == chunks - 1)
        def _():
            lax.fori_loop(0, blocks, lambda n, _: swap_start(2, n, (1,)) or 0, 0)

        reduce(i)
        return 0

    lax.fori_loop(0, chunks + lines, turn, 0)

    def close(j, _):
        exchanged(j).wait()
        cols = pl.ds(pl.multiple_of(j * span, span), span)
        mixed[:, cols] = (sums[j, z, d].astype(F32) + other[j].astype(F32)).astype(BF16)

        gone = sums.at[j, pl.ds(0, lines - 1)]
        remote(gone, gone, r_send.at[j], m_recv.at[j], e, 1 - d).wait_send()
        gone = outs.at[j, pl.ds(1, 3)]
        remote(gone, gone, b_send.at[j], m_recv.at[j], e, 1 - d).wait_send()
        return 0

    lax.fori_loop(0, chunks, close, 0)
    across(0).wait_send()
    across(1).wait_send()
    for n in range(3):
        keep(n, True).wait()

    for kind, (src, dst) in enumerate([(gate, got_gate), (up, got_up), (down, got_down)]):
        for n, (bit, cores) in enumerate(moves):
            copy = remote(
                src.at[0], dst.at[bit], s_send.at[kind, n], s_recv.at[kind, n], e, 1 - d
            )
            for_cores(cores, c, copy.wait)


def layer(lines, cap, moves, key, bits, tokens, gain, ids_t, parts_t, gate, up, down):
    rows, width = tokens.shape
    top = ids_t.shape[0]
    lanes = -(-rows // 128) * 128
    blocks = 2 * lines
    half, inner = gate.shape[1:]
    chunks = 4
    span = width // chunks
    tile = span
    part = (chunks, lines, 2, rows, span)
    sem = pltpu.SemaphoreType.DMA
    return pl.pallas_call(
        functools.partial(layer_kernel, lines, cap, chunks, lanes, moves),
        name="layer",
        out_shape=(
            jax.ShapeDtypeStruct((rows, width), BF16),
            jax.ShapeDtypeStruct((bits + 1, half, inner), BF16),
            jax.ShapeDtypeStruct((bits + 1, half, inner), BF16),
            jax.ShapeDtypeStruct((bits + 1,) + down.shape[1:], BF16),
        ),
        in_specs=[INV, INV, INV, INV, ANY, ANY, ANY],
        out_specs=(INV, ANY, ANY, ANY),
        scratch_shapes=[
            pltpu.VMEM((rows, width), BF16),
            pltpu.VMEM((2 * top, lanes), BF16),
            pltpu.VMEM((2, half, inner), BF16),
            pltpu.VMEM(down.shape[1:], BF16),
            pltpu.VMEM((lines, 2, rows, width), BF16),
            pltpu.VMEM((lines, 2, 2 * top, lanes), BF16),
            pltpu.VMEM((blocks, 3, cap, width), BF16),
            pltpu.VMEM((4, lines, 2, cap, width), BF16),
            pltpu.VMEM((lines, 2, lanes, 4 * cap), BF16),
            pltpu.VMEM((2, 2, half, inner), BF16),
            pltpu.VMEM((chunks, 2, down.shape[1], span), BF16),
            pltpu.VMEM((4, blocks * cap, inner), F32),
            pltpu.VMEM((4, blocks * cap, inner), BF16),
            pltpu.VMEM((chunks, 4, lines, 2, cap, span), BF16),
            pltpu.VMEM((chunks, lines, 2, 4, cap, span), BF16),
            pltpu.VMEM(part, BF16),
            pltpu.VMEM(part, BF16),
            pltpu.VMEM(part, BF16),
            pltpu.VMEM((rows, tile), F32),
            pltpu.VMEM((chunks, rows, span), BF16),
            sem((3,)),
            sem((4 + chunks,)),
            sem((4 + chunks,)),
            sem((4 + chunks,)),
            sem((lines + 1, 2, 2)),
            sem((lines, 2, 2)),
            sem,
            sem,
            sem((chunks,)),
            sem((chunks,)),
            sem((chunks, lines)),
            sem((chunks,)),
            sem((chunks, lines + 1)),
            sem((chunks,)),
            sem((chunks,)),
            sem((3, len(moves))),
            sem((3, len(moves))),
        ],
        compiler_params=pltpu.CompilerParams(
            collective_id=key, has_side_effects=True, vmem_limit_bytes=60 << 20
        ),
    )(tokens, gain, ids_t, parts_t, gate, up, down)


def distant_kernel(
    classes, gate, up, down, far_gate, far_up, far_down, near, send, recv, r_send, r_recv
):
    e, d = lax.axis_index("expert"), lax.axis_index("dp")
    barrier = pltpu.get_barrier_semaphore()
    bit = classes[0][0]
    to = flip(e, 1 << bit)
    mine = jnp.bool_(False)
    for _, core, low in classes:
        mine = jnp.logical_or(mine, jnp.logical_and(e % 2 == core, e // 4 % 2 == low))

    def copies():
        return [
            remote(src.at[0], dst, send.at[n], recv.at[n], to, d)
            for n, (src, dst) in enumerate([(gate, far_gate), (up, far_up), (down, far_down)])
        ]

    @pl.when(mine)
    def _():
        pl.semaphore_signal(barrier, inc=1, device_id=(to, d), device_id_type=MESH)
        pl.semaphore_wait(barrier, 1)
        for copy in copies():
            copy.start()
        for copy in copies():
            copy.wait()


RELAYS = 8


def lone_kernel(
    bit, core, low, side, gate, up, down, far_gate, far_up, far_down, near,
    send, recv, r_send, r_recv,
):
    e, d = lax.axis_index("expert"), lax.axis_index("dp")
    barrier = pltpu.get_barrier_semaphore()
    mate, helper = flip(e, 1 << bit), flip(e, 2)
    size = gate.shape[1] // RELAYS
    involved = jnp.logical_and(e % 2 == core, e // 4 % 2 == low)
    end = e // 2 % 2 == side

    def hop(n, p):
        lot = pl.ds(pl.multiple_of(p * size, size), size)
        src = [gate.at[0, lot], near.at[lot], far_gate.at[lot]][n]
        dst = [near.at[lot], far_gate.at[lot], far_gate.at[lot]][n]
        to = [helper, mate, helper][n]
        return remote(src, dst, r_send.at[n], r_recv.at[n, p], to, d)

    def every(act):
        def one(p, _):
            act(p)
            return 0

        lax.fori_loop(0, RELAYS, one, 0)

    def straight():
        return [
            remote(src.at[0], dst, send.at[n], recv.at[n], mate, d)
            for n, (src, dst) in enumerate([(up, far_up), (down, far_down)])
        ]

    def sent(n):
        remote(far_gate, far_gate, r_send.at[n], r_recv.at[n, 0], mate, d).wait_send()

    def ends():
        every(lambda p: hop(0, p).start())
        for copy in straight():
            copy.start()
        every(lambda p: hop(2, p).wait_recv())
        for copy in straight():
            copy.wait()
        sent(0)

    def helps():
        def one(p, _):
            @pl.when(p < RELAYS)
            def _():
                hop(0, p).wait_recv()
                hop(1, p).start()

            @pl.when(p > 0)
            def _():
                hop(1, p - 1).wait_recv()
                hop(2, p - 1).start()

            return 0

        lax.fori_loop(0, RELAYS + 1, one, 0)
        sent(1)
        sent(2)

    @pl.when(involved)
    def _():
        for to in (mate, helper):
            pl.semaphore_signal(barrier, inc=1, device_id=(to, d), device_id_type=MESH)
        pl.semaphore_wait(barrier, 2)
        pl.when(end)(ends)
        pl.when(jnp.logical_not(end))(helps)


def distant_swap(kernel, key, gate, up, down):
    sem = pltpu.SemaphoreType.DMA
    return pl.pallas_call(
        kernel,
        name="distant",
        out_shape=tuple(jax.ShapeDtypeStruct(w.shape[1:], BF16) for w in (gate, up, down)),
        in_specs=[ANY, ANY, ANY],
        out_specs=(ANY, ANY, ANY),
        scratch_shapes=[
            pltpu.VMEM(gate.shape[1:], BF16), sem((3,)), sem((3,)), sem((3,)), sem((3, RELAYS)),
        ],
        compiler_params=pltpu.CompilerParams(collective_id=key, has_side_effects=True),
    )(gate, up, down)


def square_body(
    tokens, norm_gain, expert_ids, route_weights, gate_weight, up_weight, down_weight, pair_list
):
    count = lax.axis_size("expert")
    dp = lax.axis_size("dp")
    e, d = lax.axis_index("expert"), lax.axis_index("dp")
    per_device = gate_weight.shape[0]
    rows, top = expert_ids.shape
    width = tokens.shape[1]
    lines = count // 4
    cap = 4 * rows * top // (3 * count * per_device)
    bits = count.bit_length() - 1
    places = jnp.arange(count, dtype=jnp.int32)
    distances = jnp.bitwise_xor(pair_list, places)
    near_bits = min(3, bits)
    kinds = [[(0,), (1,), (0, 1)], [(), (0,), (1,), (0, 1)]][: near_bits - 1]
    move_sets = [
        [(0, (0, 1))] + [(n + 1, cores) for n, cores in enumerate(picked) if cores]
        for picked in itertools.product(*kinds)
    ]
    classes = [
        (bit, core, low)
        for bit in range(near_bits, bits)
        for core in range(2)
        for low in range(2)
    ]
    sides = [c + (side,) for side in range(2) for c in classes]
    marks = jnp.zeros_like(places)
    for bit in range(1, near_bits):
        mark = jnp.where(places % 2 == 0, 1, 2) << (2 * (bit - 1))
        marks = jnp.where(distances == (1 << bit), mark, marks)
    shift = 2 * (near_bits - 1)
    for n, (bit, core, low, side) in enumerate(sides):
        spot = (places % 2 == core) & (places // 4 % 2 == low) & (places // 2 % 2 == side)
        marks = jnp.where((distances == (1 << bit)) & spot, 1 << (shift + n), marks)
    place = jnp.where(distances == 0, near_bits, 0)
    for bit in range(1, near_bits):
        place = jnp.where(distances == (1 << bit), bit, place)
    place = jnp.where(distances >= (1 << near_bits), near_bits + 1, place)
    marks = marks | jnp.where(places == e, place << 16, 0)
    marks = lax.reduce(marks, jnp.int32(0), lax.bitwise_or, (0,))
    used = [marks >> (2 * n) & 3 for n in range(near_bits - 1)]
    free = jnp.where(used[-1] == 1, 1, 0)
    choice = jnp.where(used[0] == 0, free, used[0] - 1)
    if near_bits == 3:
        choice = choice * 4 + used[1]
    slot = marks >> 16
    farther_one = slot == near_bits + 1
    slot = jnp.minimum(slot, near_bits)
    pairs = marks >> shift & ((1 << len(sides)) - 1)
    only = sum(n * (pairs >> n & 1) for n in range(len(sides)))
    far_choice = (pairs | pairs >> len(classes)) & ((1 << len(classes)) - 1)
    far_choice = jnp.where(
        (pairs & (pairs - 1) == 0) & (pairs > 0), (1 << len(classes)) + only, far_choice
    )

    def run(moves, key):
        return lambda *args: layer(lines, cap, moves, key, near_bits, *args)

    mixed, got_gate, got_up, got_down = lax.switch(
        choice,
        [run(moves, key) for key, moves in enumerate(move_sets)],
        tokens, norm_gain[None], expert_ids.T, route_weights.T, gate_weight, up_weight, down_weight,
    )
    def held(got):
        return lax.dynamic_slice_in_dim(got, slot, 1, 0)

    own = (gate_weight, up_weight, down_weight)
    near = (got_gate, got_up, got_down)

    def settled(*args):
        return tuple(held(got) for got in args[3:])

    kernels = [
        functools.partial(distant_kernel, [c for n, c in enumerate(classes) if mask >> n & 1])
        for mask in range(1, 1 << len(classes))
    ] + [functools.partial(lone_kernel, *one) for one in sides]

    def fetch(kernel, key):
        return lambda *args: distant_swap(kernel, key, *args)

    def farther(*args):
        far = lax.switch(
            far_choice - 1,
            [fetch(kernel, len(move_sets) + n) for n, kernel in enumerate(kernels)],
            *args[:3],
        )
        return tuple(jnp.where(farther_one, f[None], h) for f, h in zip(far, settled(*args)))

    if classes:
        out = lax.cond(far_choice > 0, farther, settled, *own, *near)
    else:
        out = settled(*own, *near)
    return (mixed, *out)


def body(*args):
    dp, count = lax.axis_size("dp"), lax.axis_size("expert")
    per_device = args[4].shape[0]
    rows, top = args[2].shape
    square = dp == 2 and per_device == 2 and count in (8, 16) and rows * top % (3 * count) == 0
    return square_body(*args) if square else wide_body(*args)


def solution(mesh):
    in_specs = (
        P(("expert", "dp"), None),
        P(),
        P(("expert", "dp"), None),
        P(("expert", "dp"), None),
        P("expert", "dp", None),
        P("expert", "dp", None),
        P("expert", "dp", None),
        P(),
    )
    out_specs = (
        P(("expert", "dp"), None),
        P("expert", "dp", None),
        P("expert", "dp", None),
        P("expert", "dp", None),
    )
    return jax.shard_map(body, mesh=mesh, in_specs=in_specs, out_specs=out_specs, check_vma=False)
```

```python
import functools
import itertools

import jax
import jax.numpy as jnp
from jax import lax
from jax.experimental import pallas as pl
from jax.experimental.pallas import tpu as pltpu
from jax.sharding import PartitionSpec as P

F32 = jnp.float32
BF16 = jnp.bfloat16
MESH = pl.DeviceIdType.MESH
ANY = pl.BlockSpec(memory_space=pl.ANY)
INV = pl.BlockSpec(memory_space=pltpu.VMEM)


def bit_route(count, bit, cores):
    return [
        (e, e ^ (1 << bit)) for e in range(count) if e ^ (1 << bit) < count and (e & 1) in cores
    ]


def swap_branch(moves, count):
    def run(blocks, base, distance):
        arrived = [
            [lax.ppermute(b, "expert", bit_route(count, bit, cores)) for b in blocks]
            for bit, cores in moves
        ]
        out = base
        for (bit, _), got in zip(moves, arrived):
            out = [jnp.where(distance == (1 << bit), a, o) for a, o in zip(got, out)]
        return tuple(out)

    return run


def swap(blocks, base, pair_list, count, always, bits):
    mine = lax.axis_index("expert")
    places = jnp.arange(count, dtype=jnp.int32)
    distances = jnp.bitwise_xor(pair_list, places)
    distance = jnp.bitwise_xor(pair_list[mine], mine)
    choice = jnp.int32(0)
    for n, bit in enumerate(bits):
        for core in range(2):
            used = jnp.any((distances == (1 << bit)) & (places & 1 == core)).astype(jnp.int32)
            choice = choice + (used << (2 * n + core))
    branches = []
    for mask in range(1 << (2 * len(bits))):
        moves = [(bit, (0, 1)) for bit in always]
        for n, bit in enumerate(bits):
            cores = tuple(c for c in range(2) if mask >> (2 * n + c) & 1)
            if cores:
                moves.append((bit, cores))
        branches.append(swap_branch(moves, count))
    return list(lax.switch(choice, branches, list(blocks), list(base), distance))


def placing_of(ids, parity, count, per_device, capacity):
    rows = ids.shape[0]
    experts = jnp.arange(count, dtype=jnp.int32) * per_device + parity
    equal = ids[:, :, None] == experts[None, None, :]
    member = jnp.any(equal, axis=1)
    lower = jnp.tril(jnp.ones((rows, rows), BF16), -1)
    rank = jnp.dot(lower, member.astype(BF16), preferred_element_type=F32).astype(jnp.int32)
    rank = jnp.where(member, rank, -1)
    slots = jnp.arange(capacity, dtype=jnp.int32)
    hit = rank.T[:, None, :] == slots[None, :, None]
    return equal, hit


def wide_body(
    tokens, norm_gain, expert_ids, route_weights, gate_weight, up_weight, down_weight, pair_list
):
    count = lax.axis_size("expert")
    dp = lax.axis_size("dp")
    per_device = gate_weight.shape[0]
    group = per_device if dp % per_device == 0 else 1
    experts_all = count * per_device
    rows, top = expert_ids.shape
    width = tokens.shape[1]
    capacity = max(2, 4 * rows * top // (3 * experts_all))
    d = lax.axis_index("dp")
    parity = d % group

    values = tokens.astype(F32)
    scale = lax.rsqrt(jnp.mean(values * values, axis=-1, keepdims=True) + 1e-06)
    normed = (values * scale * norm_gain).astype(BF16)
    route_bf = route_weights.astype(BF16)

    def in_group(block, shift):
        if shift % group == 0:
            return block
        route = [(i, i // group * group + (i % group + shift) % group) for i in range(dp)]
        return lax.ppermute(block, "dp", route)

    token_sets = [
        (in_group(normed, s), in_group(expert_ids, s), in_group(route_bf, s)) for s in range(group)
    ]
    token_sets, weights = lax.optimization_barrier(
        (token_sets, (gate_weight, up_weight, down_weight))
    )

    def shards(weight):
        out = []
        for s in range(dp):
            sent = lax.dynamic_index_in_dim(weight, (d + s) % group, 0, keepdims=False)
            if s:
                sent = lax.ppermute(sent, "dp", [(i, (i + s) % dp) for i in range(dp)])
            out.append(sent)
        return out

    gates, ups, downs = [shards(w) for w in weights]

    outgoing, weightings = [], []
    for normed_s, ids_s, route_s in token_sets:
        equal, hit = placing_of(ids_s, parity, count, per_device, capacity)
        picked = jnp.dot(
            hit.reshape(count * capacity, rows).astype(BF16), normed_s, preferred_element_type=F32
        ).astype(BF16)
        outgoing.append(picked.reshape(count, capacity, width))
        factor = jnp.sum(jnp.where(equal, route_s[:, :, None], jnp.zeros((), BF16)), axis=1)
        weightings.append(
            jnp.where(hit, factor.T[:, None, :], jnp.zeros((), BF16)).reshape(
                count * capacity, rows
            )
        )
    outgoing = jnp.concatenate(outgoing, axis=1)
    bit_total = count.bit_length() - 1
    firsts = [gate_weight[0], up_weight[0], down_weight[0]]
    early = list(range(1, min(3, bit_total)))
    late = list(range(3, bit_total))
    outgoing, pairs = lax.optimization_barrier((outgoing, pair_list))
    received = lax.all_to_all(outgoing, "expert", split_axis=0, concat_axis=0, tiled=True)
    half_held = swap(firsts, firsts, pairs, count, [], early)
    received, half_held = lax.optimization_barrier((received, half_held))
    columns = received.reshape(count * group * capacity, width)

    def times(x, parts):
        size = parts[0].shape[0]
        total = None
        for s, part in enumerate(parts):
            at = (d - s) % dp
            piece = lax.dynamic_slice_in_dim(x, at * size, size, axis=1)
            term = jnp.dot(piece, part, preferred_element_type=F32)
            total = term if total is None else total + term
        return total

    hidden = (jax.nn.silu(times(columns, gates)) * times(columns, ups)).astype(BF16)
    expert_out = times(hidden, downs).astype(BF16)
    expert_out, pairs = lax.optimization_barrier((expert_out, pairs))
    held = swap(firsts, half_held, pairs, count, [0], late)
    returned = lax.all_to_all(
        expert_out.reshape(count, group * capacity, width),
        "expert",
        split_axis=0,
        concat_axis=0,
        tiled=True,
    )
    returned, held = lax.optimization_barrier((returned, held))
    total = None
    for s in range(group):
        part = returned[:, s * capacity : (s + 1) * capacity].reshape(count * capacity, width)
        mix = jnp.einsum("sr,sd->rd", weightings[s], part, preferred_element_type=F32)
        if s:
            mix = in_group(mix.astype(BF16), group - s).astype(F32)
        total = mix if total is None else total + mix
    return (total.astype(BF16), held[0][None], held[1][None], held[2][None])


def flip(index, step):
    return index + step * (1 - 2 * ((index // step) % 2))


def pick(table, index):
    value = jnp.int32(table[0])
    for n in range(1, len(table)):
        value = value + jnp.int32(table[n] - table[0]) * (1 - jnp.minimum(jnp.abs(index - n), 1))
    return value


def near_first(places):
    return [sorted(range(places), key=lambda p: (abs(p - at), p)) for at in range(places)]


def greet(lines, z, e, d):
    barrier = pltpu.get_barrier_semaphore()

    def signal(to_e, to_d):
        pl.semaphore_signal(barrier, inc=1, device_id=(to_e, to_d), device_id_type=MESH)

    signal(e, 1 - d)
    for offset in range(1, 4):
        signal(beside(e, offset), d)
    total = 4 + jnp.minimum(z, 1) + jnp.minimum(lines - 1 - z, 1)

    @pl.when(z > 0)
    def _():
        signal(e - 4, d)

    @pl.when(z < lines - 1)
    def _():
        signal(e + 4, d)

    return total


def beside(e, offset):
    for bit in range(2):
        if offset >> bit & 1:
            e = flip(e, 1 << bit)
    return e


def remote(src, dst, send, recv, to_e, to_d):
    return pltpu.make_async_remote_copy(
        src_ref=src,
        dst_ref=dst,
        send_sem=send,
        recv_sem=recv,
        device_id=(to_e, to_d),
        device_id_type=MESH,
    )


def for_cores(cores, c, act):
    if len(cores) == 2:
        act()
    else:
        pl.when(c == cores[0])(act)


def layer_kernel(
    lines, cap, chunks, lanes, moves, tokens, gain, ids_t, parts_t, gate, up, down,
    mixed, got_gate, got_up, got_down,
    block, meta, stage_in, stage_out, held, metas, chosen, taken, mats, inward, all_down, gates, hidden,
    outs, back, sums, from_left, from_right, total, other,
    k_sem, o_sem, y_send, y_recv, z_send, z_recv, x_send, x_recv,
    b_sem, b_send, b_recv, r_send, r_recv, m_send, m_recv, s_send, s_recv,
):
    e, d = lax.axis_index("expert"), lax.axis_index("dp")
    z, c = e // 4, e % 2
    rows, width = tokens.shape
    top = ids_t.shape[0]
    blocks = 2 * lines
    spare = got_gate.shape[0] - 1
    span = width // chunks
    tile = span
    order = near_first(lines)
    total_greetings = greet(lines, z, e, d)
    values = tokens[...].astype(F32)
    scale = lax.rsqrt(jnp.mean(values * values, axis=-1, keepdims=True) + 1e-06)
    block[...] = (values * scale * gain[...]).astype(BF16)
    meta[...] = jnp.full(meta.shape, -1, BF16)
    tags = jnp.concatenate([ids_t[...].astype(F32), parts_t[...]], axis=0)
    meta[:, :rows] = tags.astype(BF16)
    pl.semaphore_wait(pltpu.get_barrier_semaphore(), total_greetings)

    def across(n):
        pairs = [
            (held.at[z, d], held.at[z, d]),
            (meta, metas.at[z, d]),
            (gate.at[1 - d], inward.at[0, d]),
            (up.at[1 - d], inward.at[1, d]),
        ]
        return remote(*pairs[n], y_send.at[n], y_recv.at[n], e, 1 - d)

    def own(n):
        pairs = [
            (block, held.at[z, d]),
            (meta, metas.at[z, d]),
            (gate.at[d], inward.at[0, d]),
            (up.at[d], inward.at[1, d]),
        ]
        src, dst = pairs[n]
        return pltpu.make_async_copy(src, dst, o_sem.at[n])

    def lower(j, at):
        cols = pl.ds(pl.multiple_of(j * span, span), span)
        return down.at[at, :, cols], all_down.at[j, d]

    def across_lower(j):
        return remote(*lower(j, 1 - d), y_send.at[4 + j], y_recv.at[4 + j], e, 1 - d)

    def own_lower(j):
        return pltpu.make_async_copy(*lower(j, d), o_sem.at[4 + j])

    def keep(n, out):
        src = [gate, up, down][n].at[0]
        dst = [got_gate, got_up, got_down][n].at[spare]
        stage = [stage_in.at[0], stage_in.at[1], stage_out][n]
        pair = (stage, dst) if out else (src, stage)
        return pltpu.make_async_copy(*pair, k_sem.at[n])

    def every(act):
        def one(j, _):
            act(j)
            return 0

        lax.fori_loop(0, chunks, one, 0)

    for n in range(2):
        own(n).start()
    for n in range(2):
        own(n).wait()
    for n in range(4):
        across(n).start()
    every(lambda j: across_lower(j).start())
    for n in range(3):
        keep(n, False).start()

    last = jnp.minimum(lines - 1 - z, 1)
    ahead = e - 4 + 8 * last
    behind = e + 4 - 8 * jnp.minimum(z, 1)

    def further(at, centre):
        return at + (lines - at) * (1 - jnp.minimum(jnp.abs(at - centre), 1))

    def along(way, at, dd):
        to = ahead if way else behind
        slot = at if way else further(at, z)
        return [
            remote(
                ref.at[at, dd], ref.at[at, dd],
                z_send.at[slot, dd, n], z_recv.at[at, dd, n], to, d,
            )
            for n, ref in enumerate([held, metas])
        ]

    def sideways(at, dd, n):
        return [
            remote(
                chosen.at[n, offset - 1],
                taken.at[offset, at, dd],
                x_send,
                x_recv,
                beside(e, offset),
                d,
            )
            for offset in range(1, 4)
        ]

    def swaps(kind, part):
        src = [gate, up, down][kind]
        dst = [got_gate, got_up, got_down][kind]
        size = src.shape[1] // blocks
        lot = pl.ds(pl.multiple_of(part * size, size), size)
        return [
            (
                remote(
                    src.at[0, lot], dst.at[bit, lot],
                    s_send.at[kind, n], s_recv.at[kind, n],
                    flip(e, 1 << bit), d,
                ),
                bit,
                cores,
            )
            for n, (bit, cores) in enumerate(moves)
        ]

    def swap_start(kind, part, bits):
        for copy, bit, cores in swaps(kind, part):
            if bit in bits:
                for_cores(cores, c, copy.start)

    upper = (
        lax.broadcasted_iota(jnp.int32, (lanes, lanes), 0)
        < lax.broadcasted_iota(jnp.int32, (lanes, lanes), 1)
    ).astype(F32).astype(BF16)
    slots = lax.broadcasted_iota(jnp.int32, (cap, lanes), 0).astype(F32)
    places = lax.broadcasted_iota(jnp.int32, (8, lanes), 0)

    def place(rank):
        at = jnp.int32(0)
        for k in range(lines):
            at = at + (1 - jnp.minimum(jnp.abs(rank - k), 1)) * pick(
                [order[p][k] for p in range(lines)], z
            )
        return at

    def spread(n, _):
        at, dd = place(n // 2), (d + n % 2) % 2

        @pl.when(n == 1)
        def _():
            across(0).wait_recv()
            across(1).wait_recv()

        @pl.when(n > 1)
        def _():
            for copy in along(1, at, dd):
                copy.wait_recv()

        @pl.when(jnp.logical_and(at <= z, z < lines - 1))
        def _():
            for copy in along(1, at, dd):
                copy.start()

        @pl.when(jnp.logical_and(at >= z, z > 0))
        def _():
            for copy in along(0, at, dd):
                copy.start()

        tags = metas[at, dd].astype(F32)
        ids, parts = tags[:top], tags[top:]
        member = jnp.zeros((8, lanes), F32)
        factors = []
        for offset in range(4):
            expert = (2 * beside(e, offset) + d).astype(F32)
            same = ids == expert
            row = jnp.max(jnp.where(same, 1.0, 0.0), axis=0, keepdims=True)
            factors.append(jnp.sum(jnp.where(same, parts, 0.0), axis=0, keepdims=True))
            member = jnp.where(places == offset, row, member)
        rank = jnp.dot(member.astype(BF16), upper, preferred_element_type=F32)
        hits, mixes = [], []
        for offset in range(4):
            hit = jnp.logical_and(
                rank[offset : offset + 1] == slots, member[offset : offset + 1] > 0.5
            )
            hits.append(jnp.where(hit, 1.0, 0.0))
            mixes.append(jnp.where(hit, factors[offset], 0.0))
        hit = jnp.concatenate(hits, axis=0).astype(BF16)[:, :rows]
        mats[at, dd] = jnp.transpose(jnp.concatenate(mixes, axis=0)).astype(BF16)

        def columns(j, _):
            cols = pl.ds(pl.multiple_of(j * tile, tile), tile)
            picked = jnp.dot(
                hit, held[at, dd, :, cols], preferred_element_type=F32
            ).astype(BF16)
            taken[0, at, dd, :, cols] = picked[:cap]
            for offset in range(1, 4):
                chosen[n, offset - 1, :, cols] = picked[offset * cap : (offset + 1) * cap]
            return 0

        lax.fori_loop(0, width // tile, columns, 0)
        for copy in sideways(at, dd, n):
            copy.start()
        swap_start(0, n, (0, 1, 2))
        return 0

    lax.fori_loop(0, blocks, spread, 0)
    for n in range(2, 4):
        own(n).start()
    every(lambda j: own_lower(j).start())
    for n in range(3):
        keep(n, False).wait()
        keep(n, True).start()

    def settle(n, _):
        at, dd = place(n // 2), (d + n % 2) % 2

        @pl.when(jnp.logical_and(at <= z, z < lines - 1))
        def _():
            for copy in along(1, at, dd):
                copy.wait_send()

        @pl.when(jnp.logical_and(at >= z, z > 0))
        def _():
            for copy in along(0, at, dd):
                copy.wait_send()

        swap_start(1, n, (0, 1, 2))
        swap_start(2, n, (0, 2))
        return 0

    lax.fori_loop(0, blocks, settle, 0)
    remote(chosen, chosen, x_send, x_recv, e, 1 - d).wait_send()
    rest = taken.at[pl.ds(1, 3)]
    remote(rest, rest, x_send, x_recv, e, 1 - d).wait_recv()
    lot = blocks * cap

    inner = hidden.shape[-1]
    wide = inner // 3 if inner % 384 == 0 else inner
    tiles = inner // wide

    def project(kind, _):
        for n in range(2):

            @pl.when(kind == n)
            def _():
                own(2 + n).wait()
                across(2 + n).wait()

        def one(i, _):
            offset = i // tiles
            cols = pl.ds(pl.multiple_of(i % tiles * wide, wide), wide)
            value = jnp.dot(
                taken[offset].reshape(lot, width),
                inward[kind, :, :, cols].reshape(width, wide),
                preferred_element_type=F32,
            )

            @pl.when(kind == 0)
            def _():
                gates[offset, :, cols] = value / (1.0 + jnp.exp(-value))

            @pl.when(kind == 1)
            def _():
                hidden[offset, :, cols] = (gates[offset, :, cols] * value).astype(BF16)

            return 0

        return lax.fori_loop(0, 4 * tiles, one, 0)

    lax.fori_loop(0, 2, project, 0)
    every(lambda j: own_lower(j).wait())

    def distant(k):
        return place(lines - 1 - k)

    def local(j):
        return pltpu.make_async_copy(outs.at[j, 0], back.at[j, :, :, 0], b_sem.at[j])

    def homeward(j, at):
        return [
            remote(
                outs.at[j, offset, at],
                back.at[j, at, :, offset],
                b_send.at[j],
                b_recv.at[j, at],
                beside(e, offset),
                d,
            )
            for offset in range(1, 4)
        ]

    def reduced(way, j, at, dd, here):
        to = ahead if way else behind
        land = from_left if way else from_right
        slot = at if way else further(at, here)
        return remote(
            sums.at[j, at, dd], land.at[j, at, dd], r_send.at[j], r_recv.at[j, slot, dd], to, d
        )

    def exchanged(j):
        return remote(
            sums.at[j, z, 1 - d], other.at[j], m_send.at[j], m_recv.at[j], e, 1 - d
        )

    def produce(j):
        across_lower(j).wait()

        def one(i, _):
            offset = i // (span // tile)
            cols = pl.ds(pl.multiple_of(i % (span // tile) * tile, tile), tile)
            out = jnp.dot(
                hidden[offset],
                all_down[j, :, :, cols].reshape(inner, tile),
                preferred_element_type=F32,
            )
            outs[j, offset, :, :, :, cols] = out.astype(BF16).reshape(lines, 2, cap, tile)
            return 0

        lax.fori_loop(0, 4 * (span // tile), one, 0)
        local(j).start()

        def send(k, _):
            at = distant(k)
            for copy in homeward(j, at):
                copy.start()
            return 0

        lax.fori_loop(0, lines, send, 0)

    def reduce(i):
        def one(n, _):
            k = lines - 1 - n
            j = i - 1 - k

            @pl.when(jnp.logical_and(j >= 0, j < chunks))
            def _():
                step(j, k)

            return 0

        def step(j, k):
            @pl.when(k == 0)
            def _():
                local(j).wait()

            at = distant(k)
            come = back.at[j, at, :, pl.ds(1, 3)]
            remote(come, come, b_send.at[j], b_recv.at[j, at], e, 1 - d).wait_recv()
            left = jnp.logical_and(at >= z, z > 0)
            right = jnp.logical_and(at <= z, z < lines - 1)

            def piece(i, _):
                dd = (d + 1 + i) % 2
                total[...] = jnp.dot(
                    mats[at, dd, :rows],
                    back[j, at, dd].reshape(4 * cap, span),
                    preferred_element_type=F32,
                )

                @pl.when(left)
                def _():
                    reduced(1, j, at, dd, z).wait_recv()
                    total[...] += from_left[j, at, dd].astype(F32)

                @pl.when(right)
                def _():
                    reduced(0, j, at, dd, z).wait_recv()
                    total[...] += from_right[j, at, dd].astype(F32)

                sums[j, at, dd] = total[...].astype(BF16)

                @pl.when(at > z)
                def _():
                    reduced(1, j, at, dd, z).start()

                @pl.when(at < z)
                def _():
                    reduced(0, j, at, dd, z - 1).start()

                @pl.when(jnp.logical_and(k == lines - 1, i == 0))
                def _():
                    exchanged(j).start()

                return 0

            lax.fori_loop(0, 2, piece, 0)

        lax.fori_loop(0, lines, one, 0)

    def turn(i, _):
        @pl.when(i < chunks)
        def _():
            produce(i)

        @pl.when(i == chunks - 1)
        def _():
            lax.fori_loop(0, blocks, lambda n, _: swap_start(2, n, (1,)) or 0, 0)

        reduce(i)
        return 0

    lax.fori_loop(0, chunks + lines, turn, 0)

    def close(j, _):
        exchanged(j).wait()
        cols = pl.ds(pl.multiple_of(j * span, span), span)
        mixed[:, cols] = (sums[j, z, d].astype(F32) + other[j].astype(F32)).astype(BF16)

        gone = sums.at[j, pl.ds(0, lines - 1)]
        remote(gone, gone, r_send.at[j], m_recv.at[j], e, 1 - d).wait_send()
        gone = outs.at[j, pl.ds(1, 3)]
        remote(gone, gone, b_send.at[j], m_recv.at[j], e, 1 - d).wait_send()
        return 0

    lax.fori_loop(0, chunks, close, 0)
    across(0).wait_send()
    across(1).wait_send()
    for n in range(3):
        keep(n, True).wait()

    for kind, (src, dst) in enumerate([(gate, got_gate), (up, got_up), (down, got_down)]):
        for n, (bit, cores) in enumerate(moves):
            copy = remote(
                src.at[0], dst.at[bit], s_send.at[kind, n], s_recv.at[kind, n], e, 1 - d
            )
            for_cores(cores, c, copy.wait)


def layer(lines, cap, moves, key, bits, tokens, gain, ids_t, parts_t, gate, up, down):
    rows, width = tokens.shape
    top = ids_t.shape[0]
    lanes = -(-rows // 128) * 128
    blocks = 2 * lines
    half, inner = gate.shape[1:]
    chunks = 4
    span = width // chunks
    tile = span
    part = (chunks, lines, 2, rows, span)
    sem = pltpu.SemaphoreType.DMA
    return pl.pallas_call(
        functools.partial(layer_kernel, lines, cap, chunks, lanes, moves),
        name="layer",
        out_shape=(
            jax.ShapeDtypeStruct((rows, width), BF16),
            jax.ShapeDtypeStruct((bits + 1, half, inner), BF16),
            jax.ShapeDtypeStruct((bits + 1, half, inner), BF16),
            jax.ShapeDtypeStruct((bits + 1,) + down.shape[1:], BF16),
        ),
        in_specs=[INV, INV, INV, INV, ANY, ANY, ANY],
        out_specs=(INV, ANY, ANY, ANY),
        scratch_shapes=[
            pltpu.VMEM((rows, width), BF16),
            pltpu.VMEM((2 * top, lanes), BF16),
            pltpu.VMEM((2, half, inner), BF16),
            pltpu.VMEM(down.shape[1:], BF16),
            pltpu.VMEM((lines, 2, rows, width), BF16),
            pltpu.VMEM((lines, 2, 2 * top, lanes), BF16),
            pltpu.VMEM((blocks, 3, cap, width), BF16),
            pltpu.VMEM((4, lines, 2, cap, width), BF16),
            pltpu.VMEM((lines, 2, lanes, 4 * cap), BF16),
            pltpu.VMEM((2, 2, half, inner), BF16),
            pltpu.VMEM((chunks, 2, down.shape[1], span), BF16),
            pltpu.VMEM((4, blocks * cap, inner), F32),
            pltpu.VMEM((4, blocks * cap, inner), BF16),
            pltpu.VMEM((chunks, 4, lines, 2, cap, span), BF16),
            pltpu.VMEM((chunks, lines, 2, 4, cap, span), BF16),
            pltpu.VMEM(part, BF16),
            pltpu.VMEM(part, BF16),
            pltpu.VMEM(part, BF16),
            pltpu.VMEM((rows, tile), F32),
            pltpu.VMEM((chunks, rows, span), BF16),
            sem((3,)),
            sem((4 + chunks,)),
            sem((4 + chunks,)),
            sem((4 + chunks,)),
            sem((lines + 1, 2, 2)),
            sem((lines, 2, 2)),
            sem,
            sem,
            sem((chunks,)),
            sem((chunks,)),
            sem((chunks, lines)),
            sem((chunks,)),
            sem((chunks, lines + 1, 2)),
            sem((chunks,)),
            sem((chunks,)),
            sem((3, len(moves))),
            sem((3, len(moves))),
        ],
        compiler_params=pltpu.CompilerParams(
            collective_id=key, has_side_effects=True, vmem_limit_bytes=60 << 20
        ),
    )(tokens, gain, ids_t, parts_t, gate, up, down)


def distant_kernel(
    classes, gate, up, down, far_gate, far_up, far_down, near, send, recv, r_send, r_recv
):
    e, d = lax.axis_index("expert"), lax.axis_index("dp")
    barrier = pltpu.get_barrier_semaphore()
    bit = classes[0][0]
    to = flip(e, 1 << bit)
    mine = jnp.bool_(False)
    for _, core, low in classes:
        mine = jnp.logical_or(mine, jnp.logical_and(e % 2 == core, e // 4 % 2 == low))

    def copies():
        return [
            remote(src.at[0], dst, send.at[n], recv.at[n], to, d)
            for n, (src, dst) in enumerate([(gate, far_gate), (up, far_up), (down, far_down)])
        ]

    @pl.when(mine)
    def _():
        pl.semaphore_signal(barrier, inc=1, device_id=(to, d), device_id_type=MESH)
        pl.semaphore_wait(barrier, 1)
        for copy in copies():
            copy.start()
        for copy in copies():
            copy.wait()


RELAYS = 8


def lone_kernel(
    bit, core, low, side, gate, up, down, far_gate, far_up, far_down, near,
    send, recv, r_send, r_recv,
):
    e, d = lax.axis_index("expert"), lax.axis_index("dp")
    barrier = pltpu.get_barrier_semaphore()
    mate, helper = flip(e, 1 << bit), flip(e, 2)
    size = gate.shape[1] // RELAYS
    involved = jnp.logical_and(e % 2 == core, e // 4 % 2 == low)
    end = e // 2 % 2 == side

    def hop(n, p):
        lot = pl.ds(pl.multiple_of(p * size, size), size)
        src = [gate.at[0, lot], near.at[lot], far_gate.at[lot]][n]
        dst = [near.at[lot], far_gate.at[lot], far_gate.at[lot]][n]
        to = [helper, mate, helper][n]
        return remote(src, dst, r_send.at[n], r_recv.at[n, p], to, d)

    def every(act):
        def one(p, _):
            act(p)
            return 0

        lax.fori_loop(0, RELAYS, one, 0)

    def straight():
        return [
            remote(src.at[0], dst, send.at[n], recv.at[n], mate, d)
            for n, (src, dst) in enumerate([(up, far_up), (down, far_down)])
        ]

    def sent(n):
        remote(far_gate, far_gate, r_send.at[n], r_recv.at[n, 0], mate, d).wait_send()

    def ends():
        every(lambda p: hop(0, p).start())
        for copy in straight():
            copy.start()
        every(lambda p: hop(2, p).wait_recv())
        for copy in straight():
            copy.wait()
        sent(0)

    def helps():
        def one(p, _):
            @pl.when(p < RELAYS)
            def _():
                hop(0, p).wait_recv()
                hop(1, p).start()

            @pl.when(p > 0)
            def _():
                hop(1, p - 1).wait_recv()
                hop(2, p - 1).start()

            return 0

        lax.fori_loop(0, RELAYS + 1, one, 0)
        sent(1)
        sent(2)

    @pl.when(involved)
    def _():
        for to in (mate, helper):
            pl.semaphore_signal(barrier, inc=1, device_id=(to, d), device_id_type=MESH)
        pl.semaphore_wait(barrier, 2)
        pl.when(end)(ends)
        pl.when(jnp.logical_not(end))(helps)


def distant_swap(kernel, key, gate, up, down):
    sem = pltpu.SemaphoreType.DMA
    return pl.pallas_call(
        kernel,
        name="distant",
        out_shape=tuple(jax.ShapeDtypeStruct(w.shape[1:], BF16) for w in (gate, up, down)),
        in_specs=[ANY, ANY, ANY],
        out_specs=(ANY, ANY, ANY),
        scratch_shapes=[
            pltpu.VMEM(gate.shape[1:], BF16), sem((3,)), sem((3,)), sem((3,)), sem((3, RELAYS)),
        ],
        compiler_params=pltpu.CompilerParams(collective_id=key, has_side_effects=True),
    )(gate, up, down)


def square_body(
    tokens, norm_gain, expert_ids, route_weights, gate_weight, up_weight, down_weight, pair_list
):
    count = lax.axis_size("expert")
    dp = lax.axis_size("dp")
    e, d = lax.axis_index("expert"), lax.axis_index("dp")
    per_device = gate_weight.shape[0]
    rows, top = expert_ids.shape
    width = tokens.shape[1]
    lines = count // 4
    cap = 4 * rows * top // (3 * count * per_device)
    bits = count.bit_length() - 1
    places = jnp.arange(count, dtype=jnp.int32)
    distances = jnp.bitwise_xor(pair_list, places)
    near_bits = min(3, bits)
    kinds = [[(0,), (1,), (0, 1)], [(), (0,), (1,), (0, 1)]][: near_bits - 1]
    move_sets = [
        [(0, (0, 1))] + [(n + 1, cores) for n, cores in enumerate(picked) if cores]
        for picked in itertools.product(*kinds)
    ]
    classes = [
        (bit, core, low)
        for bit in range(near_bits, bits)
        for core in range(2)
        for low in range(2)
    ]
    sides = [c + (side,) for side in range(2) for c in classes]
    marks = jnp.zeros_like(places)
    for bit in range(1, near_bits):
        mark = jnp.where(places % 2 == 0, 1, 2) << (2 * (bit - 1))
        marks = jnp.where(distances == (1 << bit), mark, marks)
    shift = 2 * (near_bits - 1)
    for n, (bit, core, low, side) in enumerate(sides):
        spot = (places % 2 == core) & (places // 4 % 2 == low) & (places // 2 % 2 == side)
        marks = jnp.where((distances == (1 << bit)) & spot, 1 << (shift + n), marks)
    place = jnp.where(distances == 0, near_bits, 0)
    for bit in range(1, near_bits):
        place = jnp.where(distances == (1 << bit), bit, place)
    place = jnp.where(distances >= (1 << near_bits), near_bits + 1, place)
    marks = marks | jnp.where(places == e, place << 16, 0)
    marks = lax.reduce(marks, jnp.int32(0), lax.bitwise_or, (0,))
    used = [marks >> (2 * n) & 3 for n in range(near_bits - 1)]
    free = jnp.where(used[-1] == 1, 1, 0)
    choice = jnp.where(used[0] == 0, free, used[0] - 1)
    if near_bits == 3:
        choice = choice * 4 + used[1]
    slot = marks >> 16
    farther_one = slot == near_bits + 1
    slot = jnp.minimum(slot, near_bits)
    pairs = marks >> shift & ((1 << len(sides)) - 1)
    only = sum(n * (pairs >> n & 1) for n in range(len(sides)))
    far_choice = (pairs | pairs >> len(classes)) & ((1 << len(classes)) - 1)
    far_choice = jnp.where(
        (pairs & (pairs - 1) == 0) & (pairs > 0), (1 << len(classes)) + only, far_choice
    )

    def run(moves, key):
        return lambda *args: layer(lines, cap, moves, key, near_bits, *args)

    mixed, got_gate, got_up, got_down = lax.switch(
        choice,
        [run(moves, key) for key, moves in enumerate(move_sets)],
        tokens, norm_gain[None], expert_ids.T, route_weights.T, gate_weight, up_weight, down_weight,
    )
    def held(got):
        return lax.dynamic_slice_in_dim(got, slot, 1, 0)

    own = (gate_weight, up_weight, down_weight)
    near = (got_gate, got_up, got_down)

    def settled(*args):
        return tuple(held(got) for got in args[3:])

    kernels = [
        functools.partial(distant_kernel, [c for n, c in enumerate(classes) if mask >> n & 1])
        for mask in range(1, 1 << len(classes))
    ] + [functools.partial(lone_kernel, *one) for one in sides]

    def fetch(kernel, key):
        return lambda *args: distant_swap(kernel, key, *args)

    def farther(*args):
        far = lax.switch(
            far_choice - 1,
            [fetch(kernel, len(move_sets) + n) for n, kernel in enumerate(kernels)],
            *args[:3],
        )
        return tuple(jnp.where(farther_one, f[None], h) for f, h in zip(far, settled(*args)))

    if classes:
        out = lax.cond(far_choice > 0, farther, settled, *own, *near)
    else:
        out = settled(*own, *near)
    return (mixed, *out)


def body(*args):
    dp, count = lax.axis_size("dp"), lax.axis_size("expert")
    per_device = args[4].shape[0]
    rows, top = args[2].shape
    square = dp == 2 and per_device == 2 and count in (8, 16) and rows * top % (3 * count) == 0
    return square_body(*args) if square else wide_body(*args)


def solution(mesh):
    in_specs = (
        P(("expert", "dp"), None),
        P(),
        P(("expert", "dp"), None),
        P(("expert", "dp"), None),
        P("expert", "dp", None),
        P("expert", "dp", None),
        P("expert", "dp", None),
        P(),
    )
    out_specs = (
        P(("expert", "dp"), None),
        P("expert", "dp", None),
        P("expert", "dp", None),
        P("expert", "dp", None),
    )
    return jax.shard_map(body, mesh=mesh, in_specs=in_specs, out_specs=out_specs, check_vma=False)
```
